256 devices in a mesh: member: 2 (over core), space: 128 (over x, y, z).
Axes of the slice: x: 4, y: 4, z: 8, core: 2. Of those that a mesh axis runs over, the one named last changes fastest.
Arguments:
- initial_states: bfloat16 [4, 65536, 98], P('member', 'space'), may hold values from -6 to 6
- target: float32 [65536, 98], P('space'), may hold values from -6 to 6
- enc_owner: int32 [65536, 1], P('space'), may hold values from 0 to 127; in each aligned block of 512 rows (0 to 511, 512 to 1023, ...) at most 8 rows name the same one
- enc_local: int32 [65536, 1], P('space'), may hold values from 0 to 255
- dec_owner: int32 [65536, 1], P('space'), may hold values from 0 to 127; in each aligned block of 512 rows (0 to 511, 512 to 1023, ...) at most 8 rows name the same one
- dec_local: int32 [65536, 1], P('space'), may hold values from 0 to 255
- w_embed: bfloat16 [98, 1024], replicated, may hold values from -0.625 to 0.625
- w_qkv: bfloat16 [1024, 3072], replicated, may hold values from -5 to 5
- w_out: bfloat16 [1024, 1024], replicated, may hold values from -0.1875 to 0.1875
- w_decode: bfloat16 [1024, 98], replicated, may hold values from -0.1875 to 0.1875
Outputs:
- predicted_states: bfloat16 [4, 65536, 98], P('member', 'space')
- probabilistic_error: float32 [65536, 98], P('space')
The draws below stay inside these ranges and needn't reach their ends.
Inputs may be any that keep to these rules, and one draw needn't show every extreme that they name: `enc_owner`: among the rows of one device, at most 8 name the same block. `dec_owner`: among the rows of one device, at most 8 name the same block.
All inputs are finite; a program needn't handle non-finite values.
Results may differ from the reference program's by a relative error of at most 0.012.
The reference program's roundings to bfloat16 on the way count: a program that leaves them out, or rounds other values in their place, can miss the bound.
Values may be sent and summed in bfloat16 or wider, within the bound.
No kernel may reach another device: no remote copies, remote signals or barrier semaphores. Data moves between devices by JAX's collectives and lax.ppermute only.
A program may use at most 128 MiB of HBM per device.

```python
import math
import jax
import jax.numpy as jnp
import numpy as np
from jax import lax

VARS = 98
WIDTH = 1024
HEADS = 16
HEAD_DIM = 64
HALF_WIN = 128
PTS_DEV = 512
NODE_DEV = 256
MEMBERS = 4
POINTS = 65536
NODES = 32768
CAP = 8
N_SPACE = 128


def draw_w_qkv(key, part):
    base = jax.random.truncated_normal(key, -4.0, 4.0, (WIDTH, 3 * WIDTH), jnp.float32) * WIDTH ** (-0.5)
    return base.astype(jnp.bfloat16)


def set_ends(array, own_key, smallest, largest):
    dims = array.shape
    index_at = [jax.random.randint(jax.random.fold_in(own_key, axis), (), 0, dims[axis]) for axis in range(len(dims))]
    array = array.at[tuple(index_at)].set(smallest)
    longest = dims.index(max(dims))
    index_at[longest] = (index_at[longest] + 1) % dims[longest]
    return array.at[tuple(index_at)].set(largest)


def steps_of(own_key, extent, shards, low, largest):
    gain, own = 1.0, jax.random.fold_in(own_key, 6)
    for position, blocks in shards:
        heights = jnp.exp(jax.random.uniform(jax.random.fold_in(own, position), (blocks,), jnp.float32, low / len(shards), largest / len(shards)))
        gain = gain * jnp.repeat(heights, extent[position] // blocks).reshape([-1 if axis == position else 1 for axis in range(len(extent))])
    return gain


def routed_block(rng, own, number, rows, number_of, top, reach, slope):
    ranking = jax.random.permutation(rng, number_of)
    packed, ordinary = portions_of(number_of, rows * top, reach, slope, True), portions_of(number_of, rows * top, reach, slope, False)
    places = jnp.arange(number_of)

    def named(sizes, turn):
        used = int((sizes > 0).sum())
        fixed = max(1, used // 4)
        passed = fixed + (places - fixed + turn * (used - fixed)) % max(1, number_of - fixed)
        return jnp.zeros((number_of,), jnp.int32).at[ranking[jnp.where(places < fixed, places, passed)]].set(jnp.asarray(sizes, jnp.int32))

    sizes = jnp.where(number % 4 == 0, named(packed, number // 4), named(ordinary, number - number // 4 - 1))
    mixed = jax.random.permutation(jax.random.fold_in(own, 3), number_of)
    donor, taker = mixed[0:number_of // 2 * 2:2], mixed[1:number_of // 2 * 2:2]
    room = jnp.minimum(sizes[donor] - 1, reach - sizes[taker]) // 2
    room = jnp.where((donor == ranking[0]) | (taker == ranking[0]) | (sizes[taker] == 0), 0, jnp.maximum(room, 0))
    passed = jax.random.randint(jax.random.fold_in(own, 4), (number_of // 2,), 0, 1 << 20) % (room + 1)
    sizes = sizes.at[donor].add(-passed).at[taker].add(passed)
    labels = jnp.searchsorted(jnp.cumsum(sizes), jnp.arange(rows * top), side="right").astype(jnp.int32)
    grid = labels.reshape(top, rows).T
    grid = grid[jax.random.permutation(jax.random.fold_in(own, 1), rows)]
    turn = jax.random.randint(jax.random.fold_in(own, 2), (rows, 1), 0, top)
    return jnp.take_along_axis(grid, (jnp.arange(top)[None, :] + turn) % top, axis=1)


def portions_of(number_of, total, limit, lean, full):
    weights = [(1 << 20) // math.isqrt(grade ** lean) + 1 for grade in range(1, number_of + 1)]
    largest = limit if full else min(limit, max(-(-total // number_of), total * weights[0] // sum(weights)))
    least = 1 if total - largest >= number_of - 1 else 0
    counts, spare = [largest] + [least] * (number_of - 1), total - largest - least * (number_of - 1)
    while spare > 0:
        movable = [i for i in range(1, number_of) if counts[i] < largest] or [i for i in range(1, number_of) if counts[i] < limit]
        whole, left = sum([weights[i] for i in movable]), spare
        for i in movable:
            more = min(limit - counts[i], max(1, left * weights[i] // whole), spare)
            counts[i] = counts[i] + more
            spare = spare - more
    return np.array(counts)


def noise(own_key, dims, scale, most, split=(), held_as=jnp.bfloat16):
    level = steps_of(own_key, dims, split, -0.22, 0.18) if split else 1.0
    values = jax.random.normal(own_key, dims, jnp.float32) * scale * level
    return jnp.minimum(jnp.maximum(values, -most), most).astype(held_as)


def setup_inputs(seed: int = 0) -> dict:
    key_of = jax.random.split(jax.random.key(seed), 11)
    initial_states = noise(key_of[0], (MEMBERS, POINTS, VARS), 1.0, 6.0, ((0, 2), (1, 128)))
    target = noise(key_of[1], (POINTS, VARS), 1.0, 6.0, ((0, 128),), jnp.float32)
    enc_owner_keys = jax.random.split(jax.random.fold_in(key_of[2], 1), POINTS // PTS_DEV)
    enc_owner_turns = jax.random.permutation(jax.random.fold_in(key_of[2], 3), POINTS // PTS_DEV)
    enc_owner = jax.vmap(lambda own, number: routed_block(jax.random.fold_in(key_of[2], 2), own, number, PTS_DEV, N_SPACE, 1, CAP, 2))(enc_owner_keys, enc_owner_turns).reshape((POINTS, 1))
    enc_local = set_ends(jax.random.randint(key_of[3], (POINTS, 1), 0, NODE_DEV), jax.random.fold_in(key_of[3], 1), 0, NODE_DEV - 1).astype(jnp.int32)
    dec_owner_keys = jax.random.split(jax.random.fold_in(key_of[4], 1), POINTS // PTS_DEV)
    dec_owner_turns = jax.random.permutation(jax.random.fold_in(key_of[4], 3), POINTS // PTS_DEV)
    dec_owner = jax.vmap(lambda own, number: routed_block(jax.random.fold_in(key_of[4], 2), own, number, PTS_DEV, N_SPACE, 1, CAP, 2))(dec_owner_keys, dec_owner_turns).reshape((POINTS, 1))
    dec_local = set_ends(jax.random.randint(key_of[5], (POINTS, 1), 0, NODE_DEV), jax.random.fold_in(key_of[5], 1), 0, NODE_DEV - 1).astype(jnp.int32)
    w_embed = noise(key_of[6], (VARS, WIDTH), VARS ** -0.5, 0.625)
    w_qkv = draw_w_qkv(jax.random.fold_in(key_of[10], 71), 0)
    w_out = noise(key_of[8], (WIDTH, WIDTH), WIDTH ** -0.5, 0.1875)
    w_decode = noise(key_of[9], (WIDTH, VARS), WIDTH ** -0.5, 0.1875)
    return {"initial_states": initial_states, "target": target, "enc_owner": enc_owner, "enc_local": enc_local, "dec_owner": dec_owner, "dec_local": dec_local, "w_embed": w_embed, "w_qkv": w_qkv, "w_out": w_out, "w_decode": w_decode}


FAIR_ALPHA = 0.95
NORM_EPS = 1e-05

def layer_norm(attention_payload):
    average = lax.optimization_barrier(jnp.mean(attention_payload, -1, keepdims=True))
    centred = attention_payload - average
    variance = lax.optimization_barrier(jnp.mean(centred * centred, -1, keepdims=True))
    return centred * lax.rsqrt(variance + NORM_EPS)

def attend(q_block, k_block, v_block, first, node_total):
    block_len = q_block.shape[0]
    scores = jnp.einsum('ihd,jhd->hij', q_block.astype(jnp.float32), k_block.astype(jnp.float32)) * HEAD_DIM ** (-0.5)
    query_pos = first + jnp.arange(block_len, dtype=jnp.int32)
    key_pos = first - HALF_WIN + jnp.arange(k_block.shape[0], dtype=jnp.int32)
    visible = (jnp.abs(query_pos[:, None] - key_pos[None, :]) <= HALF_WIN) & (key_pos[None, :] >= 0) & (key_pos[None, :] < node_total)
    scores = jnp.where(visible[None], scores, -1e+30)
    highest = lax.optimization_barrier(jnp.max(scores, -1, keepdims=True))
    expo = jnp.exp(scores - highest)
    weights = (expo / lax.optimization_barrier(jnp.sum(expo, -1, keepdims=True))).astype(jnp.bfloat16)
    return jnp.einsum('hij,jhd->ihd', weights.astype(jnp.float32), v_block.astype(jnp.float32)).astype(jnp.bfloat16)

def window_attention(query, key_rows, value_rows):
    node_total = query.shape[0]
    padded_k = jnp.pad(key_rows, ((HALF_WIN, HALF_WIN), (0, 0), (0, 0)))
    padded_v = jnp.pad(value_rows, ((HALF_WIN, HALF_WIN), (0, 0), (0, 0)))
    blocks = node_total // NODE_DEV

    def one_block(index):
        first = index * NODE_DEV
        q_block = lax.dynamic_slice_in_dim(query, first, NODE_DEV, 0)
        k_block = lax.dynamic_slice_in_dim(padded_k, first, NODE_DEV + 2 * HALF_WIN, 0)
        v_block = lax.dynamic_slice_in_dim(padded_v, first, NODE_DEV + 2 * HALF_WIN, 0)
        return attend(q_block, k_block, v_block, first, node_total)
    result = lax.map(one_block, jnp.arange(blocks, dtype=jnp.int32))
    return result.reshape(node_total, HEADS * HEAD_DIM)

def reference(initial_states, target, enc_owner, enc_local, dec_owner, dec_local, w_embed, w_qkv, w_out, w_decode):
    enc_dest = (enc_owner[:, 0] * NODE_DEV + enc_local[:, 0]).astype(jnp.int32)
    dec_dest = (dec_owner[:, 0] * NODE_DEV + dec_local[:, 0]).astype(jnp.int32)
    edge_count = jax.ops.segment_sum(jnp.ones((POINTS,), jnp.float32), enc_dest, num_segments=NODES)
    group = math.gcd(N_SPACE, 8)
    block = PTS_DEV * group
    steps_total = POINTS // block
    result_pile = []
    for member_slice in range(MEMBERS):
        member_fields = initial_states[member_slice]

        def add_block(carry, index):
            first = index * block
            piece = lax.dynamic_slice_in_dim(member_fields, first, block, 0)
            dest_piece = lax.dynamic_slice_in_dim(enc_dest, first, block, 0)
            embedded = jax.nn.silu(jnp.dot(piece, w_embed, preferred_element_type=jnp.float32)).astype(jnp.bfloat16)
            carry = carry + jax.ops.segment_sum(embedded.astype(jnp.float32), dest_piece, num_segments=NODES)
            return (carry, None)
        summed, _ = lax.scan(add_block, jnp.zeros((NODES, WIDTH), jnp.float32), jnp.arange(steps_total, dtype=jnp.int32))
        pooled = summed / jnp.maximum(edge_count, 1.0)[:, None]
        hidden = layer_norm(pooled).astype(jnp.bfloat16)
        qkv = jnp.dot(hidden, w_qkv, preferred_element_type=jnp.float32).astype(jnp.bfloat16)
        query = qkv[:, :WIDTH].reshape(NODES, HEADS, HEAD_DIM)
        key_rows = qkv[:, WIDTH:2 * WIDTH].reshape(NODES, HEADS, HEAD_DIM)
        value_rows = qkv[:, 2 * WIDTH:].reshape(NODES, HEADS, HEAD_DIM)
        attended = window_attention(query, key_rows, value_rows)
        processed_hidden = (hidden.astype(jnp.float32) + jnp.dot(attended, w_out, preferred_element_type=jnp.float32)).astype(jnp.bfloat16)
        grid_predictions = jnp.dot(processed_hidden, w_decode, preferred_element_type=jnp.float32).astype(jnp.bfloat16)
        selected_rows = jnp.take(grid_predictions, dec_dest, axis=0)
        result_pile.append((member_fields.astype(jnp.float32) + selected_rows.astype(jnp.float32)).astype(jnp.bfloat16))
    predicted_states = jnp.stack(result_pile, 0)
    attention_payload = predicted_states.astype(jnp.float32)
    count_members = attention_payload.shape[0]
    skill = lax.optimization_barrier(jnp.mean(jnp.abs(attention_payload - target[None]), 0))
    spread = lax.optimization_barrier(jnp.sum(jnp.abs(attention_payload[:, None] - attention_payload[None, :]), (0, 1)))
    fair_eps = (1.0 - FAIR_ALPHA) / count_members
    probabilistic_error = skill - (1.0 - fair_eps) / (2.0 * count_members * (count_members - 1)) * spread
    return (predicted_states, probabilistic_error)
```

```python
import functools

import jax
import jax.numpy as jnp
from jax import lax
from jax.experimental import pallas as pl
from jax.experimental.pallas import tpu as pltpu
from jax.sharding import PartitionSpec as P

HEADS = 16
HALF_WIN = 128
NODE_DEV = 256
CAP = 8
LANES = 128

FAIR_ALPHA = 0.95
NORM_EPS = 1e-05

F32 = jnp.float32
BF16 = jnp.bfloat16
NT = (((1,), (1,)), ((), ()))
TN = (((0,), (0,)), ((), ()))
VMEM_SPEC = pl.BlockSpec(memory_space=pltpu.VMEM)
SMEM_SPEC = pl.BlockSpec(memory_space=pltpu.SMEM)


def nt_dot(a, b):
    return lax.dot_general(a, b, NT, preferred_element_type=F32)


def iota(shape, dim):
    return lax.broadcasted_iota(jnp.int32, shape, dim)


def slot_row(owner_row):
    pts = owner_row.shape[1]
    square = (pts, pts)
    wide = jnp.broadcast_to(owner_row, square)
    row_id, col_id = iota(square, 0), iota(square, 1)
    owner_col = jnp.sum(jnp.where(row_id == col_id, wide, 0), axis=1, keepdims=True)
    earlier = (owner_col == wide) & (row_id < col_id)
    rank = jnp.sum(earlier.astype(jnp.int32), axis=0, keepdims=True)
    return owner_row * CAP + rank


def pack_kernel(var_count, x_ref, eo_ref, el_ref, do_ref, dl_ref, out_ref, slot_ref, aug_ref):
    members, _, pts = x_ref.shape
    n_dest = out_ref.shape[0]
    slots = n_dest * CAP
    enc_slot = slot_row(eo_ref[...])
    dec_slot = slot_row(do_ref[...])
    slot_ref[...] = dec_slot
    slot_id = iota((slots, pts), 0)
    place = (slot_id == enc_slot).astype(F32).astype(BF16)
    request = (slot_id == dec_slot).astype(F32).astype(BF16)
    row_id = iota((LANES, pts), 0)
    enc_meta = jnp.where(row_id == var_count, el_ref[...] + 1, 0).astype(F32)
    dec_meta = jnp.where(row_id == var_count, dl_ref[...] + 1, 0).astype(F32)
    asked = nt_dot(request, dec_meta.astype(BF16))
    packed = []
    for m in range(members):
        aug_ref[...] = enc_meta if m == 0 else jnp.zeros_like(enc_meta)
        aug_ref[0:var_count, :] = x_ref[m].astype(F32)
        rows = nt_dot(place, aug_ref[...].astype(BF16))
        if m == 1:
            rows = rows + asked
        packed.append(rows.reshape(n_dest, 1, CAP, LANES))
    out_ref[...] = jnp.concatenate(packed, axis=1).astype(BF16)


def member_rows(ref, m):
    n_dest = ref.shape[0]
    return ref[:, m].astype(F32).reshape(n_dest * CAP, LANES).astype(BF16)


def encode_kernel(var_count, in_ref, w_ref, lo_ref, hi_ref, wpad_ref, pooled_ref):
    n_dest, members = in_ref.shape[:2]
    slots = n_dest * CAP
    width = w_ref.shape[1]
    nodes = NODE_DEV
    wpad_ref[...] = jnp.zeros_like(wpad_ref)
    wpad_ref[0:var_count, :] = w_ref[...].astype(F32)
    chunk = 256
    lane_id = iota((8, LANES), 1)
    pick = (lane_id == var_count).astype(F32).astype(BF16)
    node_row = nt_dot(pick, member_rows(in_ref, 0))[0:1, :]
    node_id = (iota((nodes, slots), 0) + 1).astype(F32)
    assign_f = (node_id == node_row).astype(F32)
    count = jnp.maximum(jnp.sum(assign_f, axis=1, keepdims=True), 1.0)
    assign = assign_f.astype(BF16)
    for m in range(members):
        x = member_rows(in_ref, m)

        def embed(c, carry):
            cols = pl.ds(pl.multiple_of(c * chunk, chunk), chunk)
            raw = jnp.dot(x, wpad_ref[:, cols].astype(BF16), preferred_element_type=F32)
            embedded = (raw / (1.0 + jnp.exp(-raw))).astype(BF16)
            pooled_ref[:, cols] = jnp.dot(assign, embedded, preferred_element_type=F32)
            return carry

        lax.fori_loop(0, width // chunk, embed, 0)
        pooled = pooled_ref[...] / count
        centred = pooled - jnp.mean(pooled, axis=1, keepdims=True)
        variance = jnp.mean(centred * centred, axis=1, keepdims=True)
        hidden = (centred * lax.rsqrt(variance + NORM_EPS)).astype(BF16)
        lo_ref[m] = hidden[0:HALF_WIN]
        hi_ref[m] = hidden[HALF_WIN:]


def qkv_kernel(lo_ref, hi_ref, w_ref, out_ref):
    members = lo_ref.shape[0]
    rows = jnp.concatenate([r[m] for m in range(members) for r in (lo_ref, hi_ref)], axis=0)
    acc = jnp.dot(rows, w_ref[...], preferred_element_type=F32)
    out_ref[...] = acc.astype(BF16)


def attend_kernel(
    var_count, ends_ref, qkv_ref, lo_ref, hi_ref, bef_ref, aft_ref, w_kv_ref, w_out_ref, w_dec_ref,
    in_ref, out_ref, kv_ref, att_ref, wdec_ref,
):
    n_dest, members = in_ref.shape[:2]
    slots = n_dest * CAP
    half, width = lo_ref.shape[1:]
    nodes = 2 * half
    head_dim = width // HEADS
    wdec_ref[...] = jnp.zeros_like(wdec_ref)
    wdec_ref[0:var_count, :] = w_dec_ref[...].astype(F32)
    halo = jnp.concatenate([r[m] for m in range(members) for r in (bef_ref, aft_ref)], axis=0)
    chunk = 512

    def project(c, carry):
        src = pl.ds(pl.multiple_of(width + c * chunk, chunk), chunk)
        cols = pl.ds(pl.multiple_of(c * chunk, chunk), chunk)
        kv_ref[:, cols] = jnp.dot(halo, w_kv_ref[:, src], preferred_element_type=F32).astype(BF16)
        return carry

    lax.fori_loop(0, 2 * width // chunk, project, 0)

    first = ends_ref[0]
    last = ends_ref[1]
    row_id, col_id = iota((half, half), 0), iota((half, half), 1)
    big = 4 * half
    left_lo = col_id >= row_id + first * big
    left_hi = col_id >= row_id
    right_lo = col_id <= row_id
    right_hi = col_id + last * big <= row_id
    even = iota((half, LANES), 1) < head_dim
    scale = head_dim ** (-0.5)

    for m in range(members):
        base = m * nodes

        def heads(p, carry):
            q_cols = pl.ds(pl.multiple_of(p * LANES, LANES), LANES)
            k_cols = pl.ds(pl.multiple_of(width + p * LANES, LANES), LANES)
            v_cols = pl.ds(pl.multiple_of(2 * width + p * LANES, LANES), LANES)
            hv_cols = pl.ds(pl.multiple_of(width + p * LANES, LANES), LANES)
            k_own = qkv_ref[base : base + nodes, k_cols]
            v_own = qkv_ref[base : base + nodes, v_cols]
            k_bef, k_aft = kv_ref[base : base + half, q_cols], kv_ref[base + half : base + nodes, q_cols]
            v_bef, v_aft = kv_ref[base : base + half, hv_cols], kv_ref[base + half : base + nodes, hv_cols]
            for side in range(2):
                q_pair = qkv_ref[base + side * half : base + (side + 1) * half, q_cols]
                if side == 0:
                    keys = jnp.concatenate([k_bef, k_own], axis=0)
                    values = jnp.concatenate([v_bef, v_own], axis=0)
                    left, right = left_lo, right_lo
                else:
                    keys = jnp.concatenate([k_own, k_aft], axis=0)
                    values = jnp.concatenate([v_own, v_aft], axis=0)
                    left, right = left_hi, right_hi
                pair = []
                for h in range(2):
                    mine = even if h == 0 else ~even
                    q = jnp.where(mine, q_pair, jnp.zeros_like(q_pair))
                    s = nt_dot(q, keys) * scale
                    s0 = jnp.where(left, s[:, 0:half], -1e30)
                    s1 = s[:, half : 2 * half]
                    s2 = jnp.where(right, s[:, 2 * half :], -1e30)
                    top = jnp.max(jnp.maximum(jnp.maximum(s0, s1), s2), axis=1, keepdims=True)
                    e0, e1, e2 = jnp.exp(s0 - top), jnp.exp(s1 - top), jnp.exp(s2 - top)
                    inv = 1.0 / jnp.sum(e0 + e1 + e2, axis=1, keepdims=True)
                    weights = jnp.concatenate([e0 * inv, e1 * inv, e2 * inv], axis=1).astype(BF16)
                    pair.append(jnp.dot(weights, values, preferred_element_type=F32))
                att_ref[base + side * half : base + (side + 1) * half, q_cols] = jnp.where(
                    even, pair[0], pair[1]
                ).astype(BF16)
            return carry

        lax.fori_loop(0, HEADS // 2, heads, 0)

    node_lane = (iota((slots, nodes), 1) + 1).astype(F32)
    asked = in_ref[:, 1].astype(F32).reshape(slots, LANES)[:, var_count : var_count + 1]
    reply = (node_lane == asked).astype(F32).astype(BF16)
    wdec = wdec_ref[...].astype(BF16)
    packed = []
    for m in range(members):
        base = m * nodes
        hidden = jnp.concatenate([lo_ref[m], hi_ref[m]], axis=0).astype(F32)
        mixed = jnp.dot(att_ref[base : base + nodes, :], w_out_ref[...], preferred_element_type=F32)
        processed = (hidden + mixed).astype(BF16)
        decoded = nt_dot(processed, wdec).astype(BF16)
        rows = jnp.dot(reply, decoded, preferred_element_type=F32)
        packed.append(rows.reshape(n_dest, 1, CAP, LANES))
    out_ref[...] = jnp.concatenate(packed, axis=1).astype(BF16)


def predict_kernel(var_count, slot_ref, back_ref, x_ref, out_ref):
    n_dest, members = back_ref.shape[:2]
    slots = n_dest * CAP
    pts = x_ref.shape[2]
    place = (iota((slots, pts), 0) == slot_ref[...]).astype(F32).astype(BF16)
    for m in range(members):
        rows = member_rows(back_ref, m)
        got = lax.dot_general(rows, place, TN, preferred_element_type=F32)
        out_ref[m] = (x_ref[m].astype(F32) + got[0:var_count]).astype(BF16)


def score_kernel(mine_ref, other_ref, target_ref, out_ref):
    fields = [r[m].astype(F32) for r in (mine_ref, other_ref) for m in range(mine_ref.shape[0])]
    count = len(fields)
    target = target_ref[...]
    skill = sum(jnp.abs(f - target) for f in fields) / count
    spread = 2.0 * sum(
        jnp.abs(fields[i] - fields[j]) for i in range(count) for j in range(i + 1, count)
    )
    fair_eps = (1.0 - FAIR_ALPHA) / count
    out_ref[...] = skill - (1.0 - fair_eps) / (2.0 * count * (count - 1)) * spread


def params(mib=32):
    return pltpu.CompilerParams(vmem_limit_bytes=mib << 20)


def on_device(
    initial_states,
    target,
    enc_owner,
    enc_local,
    dec_owner,
    dec_local,
    w_embed,
    w_qkv,
    w_out,
    w_decode,
):
    n_space = lax.axis_size("space")
    me = lax.axis_index("space")
    members, pts, var_count = initial_states.shape
    width = w_embed.shape[1]
    nodes, half = NODE_DEV, HALF_WIN
    slots = n_space * CAP
    states = jnp.transpose(initial_states, (0, 2, 1))
    rows = [a.reshape(1, pts) for a in (enc_owner, enc_local, dec_owner, dec_local)]
    wire = jax.ShapeDtypeStruct((n_space, members, CAP, LANES), BF16)

    outgoing, dec_slot = pl.pallas_call(
        functools.partial(pack_kernel, var_count),
        out_shape=(wire, jax.ShapeDtypeStruct((1, pts), jnp.int32)),
        scratch_shapes=[pltpu.VMEM((LANES, pts), F32)],
        compiler_params=params(),
        name="pack",
    )(states, *rows)
    arrived = lax.all_to_all(outgoing, "space", 0, 0, tiled=True)

    half_shape = jax.ShapeDtypeStruct((members, half, width), BF16)
    lo, hi = pl.pallas_call(
        functools.partial(encode_kernel, var_count),
        out_shape=(half_shape, half_shape),
        scratch_shapes=[pltpu.VMEM((LANES, width), F32), pltpu.VMEM((nodes, width), F32)],
        compiler_params=params(),
        name="encode",
    )(arrived, w_embed)

    up = [(i, (i + 1) % n_space) for i in range(n_space)]
    down = [(j, i) for i, j in up]
    before = lax.ppermute(hi, "space", up)
    after = lax.ppermute(lo, "space", down)

    step = 512
    qkv = pl.pallas_call(
        qkv_kernel,
        grid=(3 * width // step,),
        in_specs=[
            pl.BlockSpec((members, half, width), lambda c: (0, 0, 0)),
            pl.BlockSpec((members, half, width), lambda c: (0, 0, 0)),
            pl.BlockSpec((width, step), lambda c: (0, c)),
        ],
        out_specs=pl.BlockSpec((members * nodes, step), lambda c: (0, c)),
        out_shape=jax.ShapeDtypeStruct((members * nodes, 3 * width), BF16),
        cost_estimate=pl.CostEstimate(
            flops=2 * members * nodes * width * 3 * width, bytes_accessed=10 << 20, transcendentals=0
        ),
        compiler_params=params(),
        name="qkv",
    )(lo, hi, w_qkv)

    ends = jnp.stack([(me == 0), (me == n_space - 1)]).astype(jnp.int32)
    replies = pl.pallas_call(
        functools.partial(attend_kernel, var_count),
        in_specs=[SMEM_SPEC] + [VMEM_SPEC] * 9,
        out_shape=wire,
        scratch_shapes=[
            pltpu.VMEM((members * nodes, 2 * width), BF16),
            pltpu.VMEM((members * nodes, width), BF16),
            pltpu.VMEM((LANES, width), F32),
        ],
        compiler_params=params(40),
        name="attend",
    )(ends, qkv, lo, hi, before, after, w_qkv, w_out, w_decode.T, arrived)

    returned = lax.all_to_all(replies, "space", 0, 0, tiled=True)
    predicted = pl.pallas_call(
        functools.partial(predict_kernel, var_count),
        out_shape=jax.ShapeDtypeStruct((members, var_count, pts), BF16),
        compiler_params=params(),
        name="predict",
    )(dec_slot, returned, states)
    other = lax.ppermute(predicted, "member", [(0, 1), (1, 0)])
    error = pl.pallas_call(
        score_kernel,
        out_shape=jax.ShapeDtypeStruct((var_count, pts), F32),
        compiler_params=params(),
        name="score",
    )(predicted, other, target.T)
    return jnp.transpose(predicted, (0, 2, 1)), error.T


def solution(mesh):
    in_specs = (
        P("member", "space", None),
        P("space", None),
        P("space", None),
        P("space", None),
        P("space", None),
        P("space", None),
        P(),
        P(),
        P(),
        P(),
    )
    out_specs = (P("member", "space", None), P("space", None))
    return jax.shard_map(
        on_device, mesh=mesh, in_specs=in_specs, out_specs=out_specs, check_vma=False
    )
```

```python
import functools

import jax
import jax.numpy as jnp
from jax import lax
from jax.experimental import pallas as pl
from jax.experimental.pallas import tpu as pltpu
from jax.sharding import PartitionSpec as P

HEADS = 16
HALF_WIN = 128
NODE_DEV = 256
CAP = 8
LANES = 128

FAIR_ALPHA = 0.95
NORM_EPS = 1e-05

F32 = jnp.float32
BF16 = jnp.bfloat16
NT = (((1,), (1,)), ((), ()))
TN = (((0,), (0,)), ((), ()))
VMEM_SPEC = pl.BlockSpec(memory_space=pltpu.VMEM)
SMEM_SPEC = pl.BlockSpec(memory_space=pltpu.SMEM)


def nt_dot(a, b):
    return lax.dot_general(a, b, NT, preferred_element_type=F32)


def iota(shape, dim):
    return lax.broadcasted_iota(jnp.int32, shape, dim)


def slot_row(owner_row):
    pts = owner_row.shape[1]
    square = (pts, pts)
    wide = jnp.broadcast_to(owner_row, square)
    row_id, col_id = iota(square, 0), iota(square, 1)
    owner_col = jnp.sum(jnp.where(row_id == col_id, wide, 0), axis=1, keepdims=True)
    earlier = (owner_col == wide) & (row_id < col_id)
    rank = jnp.sum(earlier.astype(jnp.int32), axis=0, keepdims=True)
    return owner_row * CAP + rank


def pack_kernel(var_count, x_ref, eo_ref, el_ref, do_ref, dl_ref, out_ref, slot_ref, aug_ref):
    members, _, pts = x_ref.shape
    n_dest = out_ref.shape[0]
    slots = n_dest * CAP
    enc_slot = slot_row(eo_ref[...])
    dec_slot = slot_row(do_ref[...])
    slot_ref[...] = dec_slot
    slot_id = iota((slots, pts), 0)
    place = (slot_id == enc_slot).astype(F32).astype(BF16)
    request = (slot_id == dec_slot).astype(F32).astype(BF16)
    row_id = iota((LANES, pts), 0)
    enc_meta = jnp.where(row_id == var_count, el_ref[...] + 1, 0).astype(F32)
    dec_meta = jnp.where(row_id == var_count, dl_ref[...] + 1, 0).astype(F32)
    asked = nt_dot(request, dec_meta.astype(BF16))
    packed = []
    for m in range(members):
        aug_ref[...] = enc_meta if m == 0 else jnp.zeros_like(enc_meta)
        aug_ref[0:var_count, :] = x_ref[m].astype(F32)
        rows = nt_dot(place, aug_ref[...].astype(BF16))
        if m == 1:
            rows = rows + asked
        packed.append(rows.reshape(n_dest, 1, CAP, LANES))
    out_ref[...] = jnp.concatenate(packed, axis=1).astype(BF16)


def member_rows(ref, m):
    n_dest = ref.shape[0]
    return ref[:, m].astype(F32).reshape(n_dest * CAP, LANES).astype(BF16)


def encode_kernel(var_count, m, in_ref, w_ref, lo_ref, hi_ref, pooled_ref):
    n_dest = in_ref.shape[0]
    slots = n_dest * CAP
    width = w_ref.shape[1]
    nodes = NODE_DEV
    chunk = 256
    lane_id = iota((8, LANES), 1)
    pick = (lane_id == var_count).astype(F32).astype(BF16)
    node_row = nt_dot(pick, member_rows(in_ref, 0))[0:1, :]
    node_id = (iota((nodes, slots), 0) + 1).astype(F32)
    assign_f = (node_id == node_row).astype(F32)
    share = 1.0 / jnp.maximum(jnp.sum(assign_f, axis=1, keepdims=True), 1.0)
    assign = assign_f.astype(BF16)
    x = member_rows(in_ref, m)[:, 0:var_count]

    def embed(c, carry):
        cols = pl.ds(pl.multiple_of(c * chunk, chunk), chunk)
        raw = 0.5 * jnp.dot(x, w_ref[:, cols], preferred_element_type=F32)
        embedded = (raw + raw * jnp.tanh(raw)).astype(BF16)
        pooled_ref[:, cols] = jnp.dot(assign, embedded, preferred_element_type=F32)
        return carry

    lax.fori_loop(0, width // chunk, embed, 0)
    step = 32
    for out_ref, first in ((lo_ref, 0), (hi_ref, HALF_WIN)):
        for r in range(0, HALF_WIN, step):
            part = slice(first + r, first + r + step)
            pooled = pooled_ref[part, :] * share[part]
            centred = pooled - jnp.mean(pooled, axis=1, keepdims=True)
            variance = jnp.mean(centred * centred, axis=1, keepdims=True)
            out_ref[r : r + step, :] = (centred * lax.rsqrt(variance + NORM_EPS)).astype(BF16)


def qkv_kernel(halves, *refs):
    hidden_refs, w_ref, qk_ref, vt_ref = refs[:halves], refs[halves], refs[halves + 1], refs[halves + 2]
    c = pl.program_id(0)
    rows = jnp.concatenate([r[...] for r in hidden_refs], axis=0)
    acc = jnp.dot(rows, w_ref[...], preferred_element_type=F32).astype(BF16)

    @pl.when(c < 4)
    def _():
        qk_ref[...] = acc

    @pl.when(c >= 4)
    def _():
        vt_ref[...] = acc.T


def attend_kernel(
    var_count, m, ends_ref, qk_ref, vt_ref, lo_ref, hi_ref, bef_ref, aft_ref, w_kv_ref, w_out_ref,
    w_dec_ref, *rest,
):
    if m == 0:
        out_ref, kh_ref, vth_ref, att_ref, proc_ref, left_ref, right_ref = rest
    else:
        dec_ref, in_ref, out_ref, kh_ref, vth_ref, att_ref, proc_ref, left_ref, right_ref = rest
    half, width = lo_ref.shape
    nodes = 2 * half
    head_dim = width // HEADS
    halo = jnp.concatenate([bef_ref[...], aft_ref[...]], axis=0)
    chunk = 256

    def project(c, carry):
        cols = pl.ds(pl.multiple_of(c * chunk, chunk), chunk)
        k_src = pl.ds(pl.multiple_of(width + c * chunk, chunk), chunk)
        v_src = pl.ds(pl.multiple_of(2 * width + c * chunk, chunk), chunk)
        kh_ref[:, cols] = jnp.dot(halo, w_kv_ref[:, k_src], preferred_element_type=F32).astype(BF16)
        vh = jnp.dot(halo, w_kv_ref[:, v_src], preferred_element_type=F32).astype(BF16)
        vth_ref[cols, :] = vh.T
        return carry

    lax.fori_loop(0, width // chunk, project, 0)

    key_id = iota((half, 2 * half), 0)
    query_id = iota((half, 2 * half), 1)
    query_id = jnp.where(query_id >= half, query_id - half, query_id)
    big = 4 * half
    zero, low = jnp.zeros((half, 2 * half), F32), jnp.full((half, 2 * half), -1e30, F32)
    left_ref[0] = jnp.where(key_id >= query_id + ends_ref[0] * big, zero, low)
    left_ref[1] = jnp.where(key_id >= query_id, zero, low)
    right_ref[0] = jnp.where(key_id <= query_id, zero, low)
    right_ref[1] = jnp.where(key_id + ends_ref[1] * big <= query_id, zero, low)
    even = iota((half, LANES), 1) < head_dim
    gain = head_dim ** (-0.5) * 1.4426950408889634
    base = m * nodes

    def heads(p, carry):
        cols = pl.ds(pl.multiple_of(p * LANES, LANES), LANES)
        k_cols = pl.ds(pl.multiple_of(width + p * LANES, LANES), LANES)
        k_own = qk_ref[base : base + nodes, k_cols]
        vt_own = vt_ref[cols, base : base + nodes]
        for side in range(2):
            row0 = side * half
            q = qk_ref[base + row0 : base + row0 + half, cols]
            none = jnp.zeros_like(q)
            q2 = jnp.concatenate([jnp.where(even, q, none), jnp.where(even, none, q)], axis=0)
            s_own = nt_dot(k_own, q2)
            s_halo = nt_dot(kh_ref[row0 : row0 + half, cols], q2)
            if side == 0:
                s0 = s_halo + left_ref[0]
                s1 = s_own[0:half]
                s2 = s_own[half:] + right_ref[0]
            else:
                s0 = s_own[0:half] + left_ref[1]
                s1 = s_own[half:]
                s2 = s_halo + right_ref[1]
            top = jnp.max(jnp.maximum(jnp.maximum(s0, s1), s2), axis=0, keepdims=True)
            e0, e1, e2 = (jnp.exp2((s - top) * gain) for s in (s0, s1, s2))
            inv = 1.0 / jnp.sum(e0 + e1 + e2, axis=0, keepdims=True)
            p0, p1, p2 = ((e * inv).astype(BF16) for e in (e0, e1, e2))
            if side == 0:
                p_halo, p_own = p0, jnp.concatenate([p1, p2], axis=0)
            else:
                p_own, p_halo = jnp.concatenate([p0, p1], axis=0), p2
            out = jnp.dot(vt_own, p_own, preferred_element_type=F32)
            out += jnp.dot(vth_ref[cols, row0 : row0 + half], p_halo, preferred_element_type=F32)
            pair = jnp.concatenate([out[0:head_dim, 0:half], out[head_dim:, half:]], axis=0)
            att_ref[row0 : row0 + half, cols] = pair.T.astype(BF16)
        return carry

    lax.fori_loop(0, HEADS // 2, heads, 0)

    def mix(c, carry):
        cols = pl.ds(pl.multiple_of(c * chunk, chunk), chunk)
        mixed = jnp.dot(att_ref[...], w_out_ref[:, cols], preferred_element_type=F32)
        proc_ref[0:half, cols] = (lo_ref[:, cols].astype(F32) + mixed[0:half]).astype(BF16)
        proc_ref[half:, cols] = (hi_ref[:, cols].astype(F32) + mixed[half:]).astype(BF16)
        return carry

    lax.fori_loop(0, width // chunk, mix, 0)
    decoded = nt_dot(proc_ref[...], w_dec_ref[...]).astype(BF16)
    if m == 0:
        out_ref[...] = jnp.zeros_like(out_ref)
        out_ref[:, 0:var_count] = decoded
    else:
        n_dest = in_ref.shape[0]
        slots = n_dest * CAP
        mine_ref = att_ref.at[:, 0:LANES]
        mine_ref[...] = jnp.zeros_like(mine_ref)
        mine_ref[:, 0:var_count] = decoded
        both = jnp.concatenate([dec_ref[...], mine_ref[...]], axis=1)
        node_lane = (iota((slots, nodes), 1) + 1).astype(F32)
        asked = in_ref[:, 1].astype(F32).reshape(slots, LANES)[:, var_count : var_count + 1]
        reply = (node_lane == asked).astype(F32).astype(BF16)
        rows = jnp.dot(reply, both, preferred_element_type=F32)
        packed = [rows[:, i * LANES : (i + 1) * LANES].reshape(n_dest, 1, CAP, LANES) for i in range(2)]
        out_ref[...] = jnp.concatenate(packed, axis=1).astype(BF16)


def predict_kernel(var_count, slot_ref, back_ref, x_ref, out_ref):
    n_dest, members = back_ref.shape[:2]
    slots = n_dest * CAP
    pts = x_ref.shape[2]
    place = (iota((slots, pts), 0) == slot_ref[...]).astype(F32).astype(BF16)
    for m in range(members):
        rows = member_rows(back_ref, m)
        got = lax.dot_general(rows, place, TN, preferred_element_type=F32)
        out_ref[m] = (x_ref[m].astype(F32) + got[0:var_count]).astype(BF16)


def score_kernel(mine_ref, other_ref, target_ref, out_ref):
    fields = [r[m].astype(F32) for r in (mine_ref, other_ref) for m in range(mine_ref.shape[0])]
    count = len(fields)
    target = target_ref[...]
    skill = sum(jnp.abs(f - target) for f in fields) / count
    spread = 2.0 * sum(
        jnp.abs(fields[i] - fields[j]) for i in range(count) for j in range(i + 1, count)
    )
    fair_eps = (1.0 - FAIR_ALPHA) / count
    out_ref[...] = skill - (1.0 - fair_eps) / (2.0 * count * (count - 1)) * spread


def params(mib=32):
    return pltpu.CompilerParams(vmem_limit_bytes=mib << 20)


def cost(micros):
    return pl.CostEstimate(flops=int(micros * 7e8), bytes_accessed=1 << 20, transcendentals=0)


def on_device(
    initial_states,
    target,
    enc_owner,
    enc_local,
    dec_owner,
    dec_local,
    w_embed,
    w_qkv,
    w_out,
    w_decode,
):
    n_space = lax.axis_size("space")
    me = lax.axis_index("space")
    members, pts, var_count = initial_states.shape
    width = w_embed.shape[1]
    nodes, half = NODE_DEV, HALF_WIN
    slots = n_space * CAP
    states = jnp.transpose(initial_states, (0, 2, 1))
    rows = [a.reshape(1, pts) for a in (enc_owner, enc_local, dec_owner, dec_local)]
    wire = jax.ShapeDtypeStruct((n_space, members, CAP, LANES), BF16)

    outgoing, dec_slot = pl.pallas_call(
        functools.partial(pack_kernel, var_count),
        out_shape=(wire, jax.ShapeDtypeStruct((1, pts), jnp.int32)),
        scratch_shapes=[pltpu.VMEM((LANES, pts), F32)],
        compiler_params=params(),
        name="pack",
    )(states, *rows)
    arrived = lax.all_to_all(outgoing, "space", 0, 0, tiled=True)

    half_shape = jax.ShapeDtypeStruct((half, width), BF16)
    up = [(i, (i + 1) % n_space) for i in range(n_space)]
    down = [(j, i) for i, j in up]
    hidden, halos = [], []
    for m in range(members):
        lo, hi = pl.pallas_call(
            functools.partial(encode_kernel, var_count, m),
            out_shape=(half_shape, half_shape),
            scratch_shapes=[pltpu.VMEM((nodes, width), F32)],
            compiler_params=params(),
            cost_estimate=cost(3),
            name=f"encode{m}",
        )(arrived, w_embed)
        hidden += [lo, hi]
        halos.append((lax.ppermute(hi, "space", up), lax.ppermute(lo, "space", down)))

    step = 512
    half_spec = pl.BlockSpec((half, width), lambda c: (0, 0))
    qk, vt = pl.pallas_call(
        functools.partial(qkv_kernel, len(hidden)),
        grid=(3 * width // step,),
        in_specs=[half_spec] * len(hidden) + [pl.BlockSpec((width, step), lambda c: (0, c))],
        out_specs=(
            pl.BlockSpec((members * nodes, step), lambda c: (0, jnp.minimum(c, 3))),
            pl.BlockSpec((step, members * nodes), lambda c: (jnp.maximum(c - 4, 0), 0)),
        ),
        out_shape=(
            jax.ShapeDtypeStruct((members * nodes, 2 * width), BF16),
            jax.ShapeDtypeStruct((width, members * nodes), BF16),
        ),
        cost_estimate=cost(5),
        compiler_params=params(),
        name="qkv",
    )(*hidden, w_qkv)

    ends = jnp.stack([(me == 0), (me == n_space - 1)]).astype(jnp.int32)
    decoded = None
    for m in range(members):
        extra = () if m == 0 else (decoded, arrived)
        decoded = pl.pallas_call(
            functools.partial(attend_kernel, var_count, m),
            in_specs=[SMEM_SPEC] + [VMEM_SPEC] * (9 + len(extra)),
            out_shape=jax.ShapeDtypeStruct((nodes, LANES), BF16) if m == 0 else wire,
            scratch_shapes=[
                pltpu.VMEM((nodes, width), BF16),
                pltpu.VMEM((width, nodes), BF16),
                pltpu.VMEM((nodes, width), BF16),
                pltpu.VMEM((nodes, width), BF16),
                pltpu.VMEM((2, half, nodes), F32),
                pltpu.VMEM((2, half, nodes), F32),
            ],
            compiler_params=params(),
            cost_estimate=cost(8),
            name=f"attend{m}",
        )(ends, qk, vt, *hidden[2 * m : 2 * m + 2], *halos[m], w_qkv, w_out, w_decode.T, *extra)
    replies = decoded

    returned = lax.all_to_all(replies, "space", 0, 0, tiled=True)
    predicted = pl.pallas_call(
        functools.partial(predict_kernel, var_count),
        out_shape=jax.ShapeDtypeStruct((members, var_count, pts), BF16),
        compiler_params=params(),
        name="predict",
    )(dec_slot, returned, states)
    other = lax.ppermute(predicted, "member", [(0, 1), (1, 0)])
    error = pl.pallas_call(
        score_kernel,
        out_shape=jax.ShapeDtypeStruct((var_count, pts), F32),
        compiler_params=params(),
        name="score",
    )(predicted, other, target.T)
    return jnp.transpose(predicted, (0, 2, 1)), error.T


def solution(mesh):
    in_specs = (
        P("member", "space", None),
        P("space", None),
        P("space", None),
        P("space", None),
        P("space", None),
        P("space", None),
        P(),
        P(),
        P(),
        P(),
    )
    out_specs = (P("member", "space", None), P("space", None))
    return jax.shard_map(
        on_device, mesh=mesh, in_specs=in_specs, out_specs=out_specs, check_vma=False
    )
```

```python
import functools

import jax
import jax.numpy as jnp
from jax import lax
from jax.experimental import pallas as pl
from jax.experimental.pallas import tpu as pltpu
from jax.sharding import PartitionSpec as P

HEADS = 16
HALF_WIN = 128
NODE_DEV = 256
CAP = 8
LANES = 128
GRID = (4, 4, 8)

FAIR_ALPHA = 0.95
NORM_EPS = 1e-05

F32 = jnp.float32
BF16 = jnp.bfloat16
NT = (((1,), (1,)), ((), ()))
TN = (((0,), (0,)), ((), ()))
VMEM_SPEC = pl.BlockSpec(memory_space=pltpu.VMEM)
HBM_SPEC = pl.BlockSpec(memory_space=pltpu.HBM)
SMEM_SPEC = pl.BlockSpec(memory_space=pltpu.SMEM)


def nt_dot(a, b):
    return lax.dot_general(a, b, NT, preferred_element_type=F32)


def iota(shape, dim):
    return lax.broadcasted_iota(jnp.int32, shape, dim)


def path_place(block, dims):
    _, ny, nz = dims
    x, rest = block // (ny * nz), block % (ny * nz)
    y, z = rest // nz, rest % nz
    turn = (x * ny + y) % 2
    y = jnp.where(x % 2 == 1, ny - 1 - y, y) if not isinstance(block, int) else (ny - 1 - y if x % 2 else y)
    z = jnp.where(turn == 1, nz - 1 - z, z) if not isinstance(block, int) else (nz - 1 - z if turn else z)
    return (x * ny + y) * nz + z


def slot_row(owner_row):
    pts = owner_row.shape[1]
    square = (pts, pts)
    wide = jnp.broadcast_to(owner_row, square)
    row_id, col_id = iota(square, 0), iota(square, 1)
    owner_col = jnp.sum(jnp.where(row_id == col_id, wide, 0), axis=1, keepdims=True)
    earlier = (owner_col == wide) & (row_id < col_id)
    rank = jnp.sum(earlier.astype(jnp.int32), axis=0, keepdims=True)
    return path_place(owner_row, GRID) * CAP + rank


def pack_kernel(
    var_count, x_ref, eo_hbm, el_hbm, do_hbm, dl_hbm, w_hbm, out_ref, slot_ref, w_ref,
    eo_ref, el_ref, do_ref, dl_ref, aug_ref, sems,
):
    members, _, pts = x_ref.shape
    n_dest = out_ref.shape[0]
    slots = n_dest * CAP
    copies = [
        pltpu.make_async_copy(src, dst, sems.at[i])
        for i, (src, dst) in enumerate(
            [(eo_hbm, eo_ref), (do_hbm, do_ref), (el_hbm, el_ref), (dl_hbm, dl_ref), (w_hbm, w_ref)]
        )
    ]
    for copy in copies:
        copy.start()
    copies[0].wait()
    enc_slot = slot_row(eo_ref[...])
    copies[1].wait()
    dec_slot = slot_row(do_ref[...])
    slot_ref[...] = dec_slot
    slot_id = iota((slots, pts), 0)
    place = (slot_id == enc_slot).astype(F32).astype(BF16)
    request = (slot_id == dec_slot).astype(F32).astype(BF16)
    row_id = iota((LANES, pts), 0)
    copies[2].wait()
    copies[3].wait()
    enc_meta = jnp.where(row_id == var_count, el_ref[...] + 1, 0).astype(F32)
    dec_meta = jnp.where(row_id == var_count, dl_ref[...] + 1, 0).astype(F32)
    asked = nt_dot(request, dec_meta.astype(BF16))
    packed = []
    for m in range(members):
        aug_ref[...] = enc_meta if m == 0 else jnp.zeros_like(enc_meta)
        aug_ref[0:var_count, :] = x_ref[m].astype(F32)
        rows = nt_dot(place, aug_ref[...].astype(BF16))
        if m == 1:
            rows = rows + asked
        packed.append(rows.reshape(n_dest, 1, CAP, LANES))
    out_ref[...] = jnp.concatenate(packed, axis=1).astype(BF16)
    copies[4].wait()


def member_rows(ref, m):
    n_dest = ref.shape[0]
    return ref[:, m].astype(F32).reshape(n_dest * CAP, LANES).astype(BF16)


def encode_kernel(var_count, m, in_ref, w_ref, lo_ref, hi_ref, pooled_ref, ea_ref, eb_ref):
    n_dest = in_ref.shape[0]
    slots = n_dest * CAP
    width = w_ref.shape[1]
    nodes = NODE_DEV
    chunk = 256
    lane_id = iota((8, LANES), 1)
    pick = (lane_id == var_count).astype(F32).astype(BF16)
    node_row = nt_dot(pick, member_rows(in_ref, 0))[0:1, :]
    node_id = (iota((nodes, slots), 0) + 1).astype(F32)
    assign_f = (node_id == node_row).astype(F32)
    share = 1.0 / jnp.maximum(jnp.sum(assign_f, axis=1, keepdims=True), 1.0)
    assign = assign_f.astype(BF16)
    x = member_rows(in_ref, m)[:, 0:var_count]

    def embed(c, e_ref):
        cols = pl.ds(pl.multiple_of(c * chunk, chunk), chunk)
        raw = 0.5 * jnp.dot(x, w_ref[:, cols], preferred_element_type=F32)
        e_ref[...] = (raw + raw * jnp.tanh(raw)).astype(BF16)

    def pool(c, e_ref):
        cols = pl.ds(pl.multiple_of(c * chunk, chunk), chunk)
        pooled_ref[:, cols] = jnp.dot(assign, e_ref[...], preferred_element_type=F32)

    chunks = width // chunk
    embed(0, ea_ref)
    for c in range(chunks):
        here, there = (ea_ref, eb_ref) if c % 2 == 0 else (eb_ref, ea_ref)
        if c + 1 < chunks:
            embed(c + 1, there)
        pool(c, here)
    step = 32
    for out_ref, first in ((lo_ref, 0), (hi_ref, HALF_WIN)):
        for r in range(0, HALF_WIN, step):
            part = slice(first + r, first + r + step)
            pooled = pooled_ref[part, :] * share[part]
            centred = pooled - jnp.mean(pooled, axis=1, keepdims=True)
            variance = jnp.mean(centred * centred, axis=1, keepdims=True)
            out_ref[r : r + step, :] = (centred * lax.rsqrt(variance + NORM_EPS)).astype(BF16)


def qkv_kernel(halves, *refs):
    hidden_refs, (w_ref, qk_ref, vt_ref, rows_ref) = refs[:halves], refs[halves:]
    width = rows_ref.shape[1]
    half = rows_ref.shape[0] // halves
    for i, ref in enumerate(hidden_refs):
        rows_ref[i * half : (i + 1) * half, :] = ref[...]
    chunk = 256

    def project(cols):
        return jnp.dot(rows_ref[...], w_ref[:, cols], preferred_element_type=F32).astype(BF16)

    @pl.loop(0, 2 * width // chunk)
    def _(c):
        cols = pl.ds(pl.multiple_of(c * chunk, chunk), chunk)
        qk_ref[:, cols] = project(cols)

    @pl.loop(0, width // chunk)
    def _(c):
        rows = pl.ds(pl.multiple_of(c * chunk, chunk), chunk)
        vt_ref[rows, :] = project(pl.ds(pl.multiple_of(2 * width + c * chunk, chunk), chunk)).T


def attend_kernel(
    var_count, m, ends_ref, qk_ref, vt_ref, lo_ref, hi_ref, bef_ref, aft_ref, w_kv_ref, w_out_ref,
    w_dec_ref, *rest,
):
    if m == 0:
        out_ref, kh_ref, vth_ref, att_ref, proc_ref, left_ref, right_ref, sa_ref, sb_ref, e_ref = rest
    else:
        dec_ref, in_ref, out_ref, kh_ref, vth_ref, att_ref, proc_ref, left_ref, right_ref, sa_ref, sb_ref, e_ref = rest
    half, width = lo_ref.shape
    nodes = 2 * half
    head_dim = width // HEADS
    proc_ref[0:half, :] = bef_ref[...]
    proc_ref[half:, :] = aft_ref[...]
    chunk = 256

    def project(c, carry):
        cols = pl.ds(pl.multiple_of(c * chunk, chunk), chunk)
        k_src = pl.ds(pl.multiple_of(width + c * chunk, chunk), chunk)
        v_src = pl.ds(pl.multiple_of(2 * width + c * chunk, chunk), chunk)
        kh_ref[:, cols] = jnp.dot(proc_ref[...], w_kv_ref[:, k_src], preferred_element_type=F32).astype(BF16)
        vh = jnp.dot(proc_ref[...], w_kv_ref[:, v_src], preferred_element_type=F32).astype(BF16)
        vth_ref[cols, :] = vh.T
        return carry

    lax.fori_loop(0, width // chunk, project, 0)

    key_id = iota((half, 2 * half), 0)
    query_id = iota((half, 2 * half), 1)
    query_id = jnp.where(query_id >= half, query_id - half, query_id)
    big = 4 * half
    zero, low = jnp.zeros((half, 2 * half), F32), jnp.full((half, 2 * half), -1e30, F32)
    left_ref[0] = jnp.where(key_id >= query_id + ends_ref[0] * big, zero, low)
    left_ref[1] = jnp.where(key_id >= query_id, zero, low)
    right_ref[0] = jnp.where(key_id <= query_id, zero, low)
    right_ref[1] = jnp.where(key_id + ends_ref[1] * big <= query_id, zero, low)
    even = iota((half, LANES), 1) < head_dim
    gain = head_dim ** (-0.5) * 1.4426950408889634
    base = m * nodes

    def scores(p, s_ref):
        cols = pl.ds(pl.multiple_of(p * LANES, LANES), LANES)
        k_cols = pl.ds(pl.multiple_of(width + p * LANES, LANES), LANES)
        k_own = qk_ref[base : base + nodes, k_cols]
        for side in range(2):
            row0 = side * half
            q = qk_ref[base + row0 : base + row0 + half, cols]
            none = jnp.zeros_like(q)
            q2 = jnp.concatenate([jnp.where(even, q, none), jnp.where(even, none, q)], axis=0)
            s_own = nt_dot(k_own, q2)
            s_halo = nt_dot(kh_ref[row0 : row0 + half, cols], q2)
            if side == 0:
                s_ref[side, 0:half] = s_own[0:half]
                s_ref[side, half:nodes] = s_own[half:] + right_ref[0]
                s_ref[side, nodes:] = s_halo + left_ref[0]
            else:
                s_ref[side, 0:half] = s_own[0:half] + left_ref[1]
                s_ref[side, half:nodes] = s_own[half:]
                s_ref[side, nodes:] = s_halo + right_ref[1]

    def finish(p, s_ref):
        cols = pl.ds(pl.multiple_of(p * LANES, LANES), LANES)
        blocks = (slice(0, half), slice(half, nodes), slice(nodes, nodes + half))
        for side in range(2):
            row0 = side * half
            s0, s1, s2 = (s_ref[side, b] for b in blocks)
            top = jnp.max(jnp.maximum(jnp.maximum(s0, s1), s2), axis=0, keepdims=True)
            total = None
            for b in blocks:
                e = jnp.exp2((s_ref[side, b] - top) * gain)
                e_ref[side, b] = e
                total = e if total is None else total + e
            inv = 1.0 / jnp.sum(total, axis=0, keepdims=True)
            p_own = (e_ref[side, 0:nodes] * inv).astype(BF16)
            p_halo = (e_ref[side, nodes:] * inv).astype(BF16)
            out = jnp.dot(vt_ref[cols, base : base + nodes], p_own, preferred_element_type=F32)
            out += jnp.dot(vth_ref[cols, row0 : row0 + half], p_halo, preferred_element_type=F32)
            pair = jnp.concatenate([out[0:head_dim, 0:half], out[head_dim:, half:]], axis=0)
            att_ref[row0 : row0 + half, cols] = pair.T.astype(BF16)

    pairs = HEADS // 2
    scores(0, sa_ref)

    def heads(i, carry):
        p = 2 * i
        scores(p + 1, sb_ref)
        finish(p, sa_ref)
        scores(jnp.minimum(p + 2, pairs - 1), sa_ref)
        finish(p + 1, sb_ref)
        return carry

    lax.fori_loop(0, pairs // 2, heads, 0)

    def mix(c, carry):
        cols = pl.ds(pl.multiple_of(c * chunk, chunk), chunk)
        mixed = jnp.dot(att_ref[...], w_out_ref[:, cols], preferred_element_type=F32)
        proc_ref[0:half, cols] = (lo_ref[:, cols].astype(F32) + mixed[0:half]).astype(BF16)
        proc_ref[half:, cols] = (hi_ref[:, cols].astype(F32) + mixed[half:]).astype(BF16)
        return carry

    lax.fori_loop(0, width // chunk, mix, 0)
    decoded = nt_dot(proc_ref[...], w_dec_ref[...]).astype(BF16)
    if m == 0:
        out_ref[...] = jnp.zeros_like(out_ref)
        out_ref[:, 0:var_count] = decoded
    else:
        n_dest = in_ref.shape[0]
        slots = n_dest * CAP
        mine_ref = att_ref.at[:, 0:LANES]
        mine_ref[...] = jnp.zeros_like(mine_ref)
        mine_ref[:, 0:var_count] = decoded
        both = jnp.concatenate([dec_ref[...], mine_ref[...]], axis=1)
        node_lane = (iota((slots, nodes), 1) + 1).astype(F32)
        asked = in_ref[:, 1].astype(F32).reshape(slots, LANES)[:, var_count : var_count + 1]
        reply = (node_lane == asked).astype(F32).astype(BF16)
        rows = jnp.dot(reply, both, preferred_element_type=F32)
        packed = [rows[:, i * LANES : (i + 1) * LANES].reshape(n_dest, 1, CAP, LANES) for i in range(2)]
        out_ref[...] = jnp.concatenate(packed, axis=1).astype(BF16)


def predict_kernel(var_count, slot_ref, back_ref, x_ref, out_ref):
    n_dest, members = back_ref.shape[:2]
    slots = n_dest * CAP
    pts = x_ref.shape[2]
    place = (iota((slots, pts), 0) == slot_ref[...]).astype(F32).astype(BF16)
    for m in range(members):
        rows = member_rows(back_ref, m)
        got = lax.dot_general(rows, place, TN, preferred_element_type=F32)
        out_ref[m] = (x_ref[m].astype(F32) + got[0:var_count]).astype(BF16)


def score_kernel(mine_ref, other_ref, target_ref, out_ref):
    fields = [r[m].astype(F32) for r in (mine_ref, other_ref) for m in range(mine_ref.shape[0])]
    count = len(fields)
    target = target_ref[...]
    skill = sum(jnp.abs(f - target) for f in fields) / count
    spread = 2.0 * sum(
        jnp.abs(fields[i] - fields[j]) for i in range(count) for j in range(i + 1, count)
    )
    fair_eps = (1.0 - FAIR_ALPHA) / count
    out_ref[...] = skill - (1.0 - fair_eps) / (2.0 * count * (count - 1)) * spread


def params(mib=32):
    return pltpu.CompilerParams(vmem_limit_bytes=mib << 20)


def cost(micros):
    return pl.CostEstimate(flops=int(micros * 7e8), bytes_accessed=1 << 20, transcendentals=0)


def on_device(
    initial_states,
    target,
    enc_owner,
    enc_local,
    dec_owner,
    dec_local,
    w_embed,
    w_qkv,
    w_out,
    w_decode,
):
    n_space = lax.axis_size("space")
    me = lax.axis_index("space")
    members, pts, var_count = initial_states.shape
    width = w_embed.shape[1]
    nodes, half = NODE_DEV, HALF_WIN
    slots = n_space * CAP
    states = jnp.transpose(initial_states, (0, 2, 1))
    rows = [a.reshape(1, pts) for a in (enc_owner, enc_local, dec_owner, dec_local)]
    wire = jax.ShapeDtypeStruct((n_space, members, CAP, LANES), BF16)

    row_shape = pltpu.VMEM((1, pts), jnp.int32)
    outgoing, dec_slot, w_enc = pl.pallas_call(
        functools.partial(pack_kernel, var_count),
        in_specs=[VMEM_SPEC] + [HBM_SPEC] * 5,
        out_shape=(
            wire,
            jax.ShapeDtypeStruct((1, pts), jnp.int32),
            jax.ShapeDtypeStruct(w_embed.shape, BF16),
        ),
        scratch_shapes=[row_shape] * 4
        + [pltpu.VMEM((LANES, pts), F32), pltpu.SemaphoreType.DMA((5,))],
        compiler_params=params(),
        cost_estimate=cost(2),
        name="pack",
    )(states, *rows, w_embed)
    at = [path_place(b, GRID) for b in range(n_space)]
    ends = jnp.stack([(me == at[0]), (me == at[-1])]).astype(jnp.int32)
    outgoing, ends = lax.optimization_barrier((outgoing, ends))
    arrived = lax.all_to_all(outgoing, "space", 0, 0, tiled=True)

    half_shape = jax.ShapeDtypeStruct((half, width), BF16)
    up = [(at[i], at[(i + 1) % n_space]) for i in range(n_space)]
    down = [(j, i) for i, j in up]
    hidden, halos = [], []
    for m in range(members):
        lo, hi = pl.pallas_call(
            functools.partial(encode_kernel, var_count, m),
            out_shape=(half_shape, half_shape),
            scratch_shapes=[pltpu.VMEM((nodes, width), F32)] + [pltpu.VMEM((slots, 256), BF16)] * 2,
            compiler_params=params(),
            cost_estimate=cost(3),
            name=f"encode{m}",
        )(arrived, w_enc)
        hidden += [lo, hi]
        halos.append((lax.ppermute(hi, "space", up), lax.ppermute(lo, "space", down)))

    qk, vt = pl.pallas_call(
        functools.partial(qkv_kernel, len(hidden)),
        out_shape=(
            jax.ShapeDtypeStruct((members * nodes, 2 * width), BF16),
            jax.ShapeDtypeStruct((width, members * nodes), BF16),
        ),
        scratch_shapes=[pltpu.VMEM((members * nodes, width), BF16)],
        cost_estimate=cost(5),
        compiler_params=params(),
        name="qkv",
    )(*hidden, w_qkv)

    decoded = None
    for m in range(members):
        extra = () if m == 0 else (decoded, arrived)
        decoded = pl.pallas_call(
            functools.partial(attend_kernel, var_count, m),
            in_specs=[SMEM_SPEC] + [VMEM_SPEC] * (9 + len(extra)),
            out_shape=jax.ShapeDtypeStruct((nodes, LANES), BF16) if m == 0 else wire,
            scratch_shapes=[
                pltpu.VMEM((nodes, width), BF16),
                pltpu.VMEM((width, nodes), BF16),
                pltpu.VMEM((nodes, width), BF16),
                pltpu.VMEM((nodes, width), BF16),
                pltpu.VMEM((2, half, nodes), F32),
                pltpu.VMEM((2, half, nodes), F32),
                pltpu.VMEM((2, nodes + half, nodes), F32),
                pltpu.VMEM((2, nodes + half, nodes), F32),
                pltpu.VMEM((2, nodes + half, nodes), F32),
            ],
            compiler_params=params(),
            cost_estimate=cost(8),
            name=f"attend{m}",
        )(ends, qk, vt, *hidden[2 * m : 2 * m + 2], *halos[m], w_qkv, w_out, w_decode.T, *extra)
    replies = decoded

    returned = lax.all_to_all(replies, "space", 0, 0, tiled=True)
    predicted = pl.pallas_call(
        functools.partial(predict_kernel, var_count),
        out_shape=jax.ShapeDtypeStruct((members, var_count, pts), BF16),
        compiler_params=params(),
        name="predict",
    )(dec_slot, returned, states)
    other = lax.ppermute(predicted, "member", [(0, 1), (1, 0)])
    error = pl.pallas_call(
        score_kernel,
        out_shape=jax.ShapeDtypeStruct((var_count, pts), F32),
        compiler_params=params(),
        name="score",
    )(predicted, other, target.T)
    return jnp.transpose(predicted, (0, 2, 1)), error.T


def solution(mesh):
    in_specs = (
        P("member", "space", None),
        P("space", None),
        P("space", None),
        P("space", None),
        P("space", None),
        P("space", None),
        P(),
        P(),
        P(),
        P(),
    )
    out_specs = (P("member", "space", None), P("space", None))
    return jax.shard_map(
        on_device, mesh=mesh, in_specs=in_specs, out_specs=out_specs, check_vma=False
    )
```

```python
import functools

import jax
import jax.numpy as jnp
from jax import lax
from jax.experimental import pallas as pl
from jax.experimental.pallas import tpu as pltpu
from jax.sharding import PartitionSpec as P

HEADS = 16
HALF_WIN = 128
NODE_DEV = 256
CAP = 8
LANES = 128
GRID = (4, 4, 8)
Y_BITS, Z_BITS = 2, 3

FAIR_ALPHA = 0.95
NORM_EPS = 1e-05

F32 = jnp.float32
BF16 = jnp.bfloat16
NT = (((1,), (1,)), ((), ()))
TN = (((0,), (0,)), ((), ()))
VMEM_SPEC = pl.BlockSpec(memory_space=pltpu.VMEM)
HBM_SPEC = pl.BlockSpec(memory_space=pltpu.HBM)


def nt_dot(a, b):
    return lax.dot_general(a, b, NT, preferred_element_type=F32)


def iota(shape, dim):
    return lax.broadcasted_iota(jnp.int32, shape, dim)


def path_place(block):
    _, ny, nz = GRID
    line, z = block >> Z_BITS, block & (nz - 1)
    x, y = line >> Y_BITS, line & (ny - 1)
    z = z + (line & 1) * (nz - 1 - 2 * z)
    y = y + (x & 1) * (ny - 1 - 2 * y)
    return (((x << Y_BITS) + y) << Z_BITS) + z


def slot_row(owner_row):
    pts = owner_row.shape[1]
    owner = owner_row.astype(F32)
    owner_col = jnp.broadcast_to(owner, (8, pts)).T[:, 0:1]
    block = LANES
    ahead = iota((block, block), 0) < iota((block, block), 1)
    ranks = []
    for c in range(0, pts, block):
        wide = jnp.broadcast_to(owner[:, c : c + block], (block, block))
        count = jnp.where(ahead & (owner_col[c : c + block] == wide), 1.0, 0.0)
        for r in range(0, c, block):
            count += jnp.where(owner_col[r : r + block] == wide, 1.0, 0.0)
        ranks.append(jnp.sum(count, axis=0, keepdims=True))
    rank = jnp.concatenate(ranks, axis=1).astype(jnp.int32)
    return path_place(owner_row) * CAP + rank


def pack_kernel(
    var_count, x_hbm, eo_hbm, el_hbm, do_hbm, dl_hbm, w_hbm, out_ref, slot_ref, w_ref, states_ref,
    x_ref, eo_ref, el_ref, do_ref, dl_ref, aug_ref, sems,
):
    members, _, pts = states_ref.shape
    n_dest = out_ref.shape[0]
    slots = n_dest * CAP
    copies = [
        pltpu.make_async_copy(src, dst, sems.at[i])
        for i, (src, dst) in enumerate(
            [(eo_hbm, eo_ref), (do_hbm, do_ref), (el_hbm, el_ref), (dl_hbm, dl_ref), (x_hbm, x_ref), (w_hbm, w_ref)]
        )
    ]
    for copy in copies:
        copy.start()
    copies[0].wait()
    enc_slot = slot_row(eo_ref[...])
    copies[1].wait()
    dec_slot = slot_row(do_ref[...])
    slot_ref[...] = dec_slot
    slot_id = iota((slots, pts), 0)
    place = (slot_id == enc_slot).astype(F32).astype(BF16)
    request = (slot_id == dec_slot).astype(F32).astype(BF16)
    row_id = iota((LANES, pts), 0)
    copies[2].wait()
    copies[3].wait()
    enc_meta = jnp.where(row_id == var_count, el_ref[...] + 1, 0).astype(F32)
    dec_meta = jnp.where(row_id == var_count, dl_ref[...] + 1, 0).astype(F32)
    asked = nt_dot(request, dec_meta.astype(BF16))
    packed = []
    copies[4].wait()
    for m in range(members):
        aug_ref[...] = enc_meta if m == 0 else jnp.zeros_like(enc_meta)
        field = x_ref[:, m, :]
        aug_ref[0:var_count, :] = field.astype(F32)
        states_ref[m] = field
        rows = nt_dot(place, aug_ref[...].astype(BF16))
        if m == 1:
            rows = rows + asked
        packed.append(rows.reshape(n_dest, 1, CAP, LANES))
    out_ref[...] = jnp.concatenate(packed, axis=1).astype(BF16)
    copies[5].wait()


def member_rows(ref, m):
    n_dest = ref.shape[0]
    return ref[:, m].astype(F32).reshape(n_dest * CAP, LANES).astype(BF16)


def encode_kernel(var_count, m, in_ref, w_ref, lo_ref, hi_ref, pooled_ref, ea_ref, eb_ref):
    n_dest = in_ref.shape[0]
    slots = n_dest * CAP
    width = w_ref.shape[1]
    nodes = NODE_DEV
    chunk = 256
    lane_id = iota((8, LANES), 1)
    pick = (lane_id == var_count).astype(F32).astype(BF16)
    node_row = nt_dot(pick, member_rows(in_ref, 0))[0:1, :]
    node_id = (iota((nodes, slots), 0) + 1).astype(F32)
    assign_f = (node_id == node_row).astype(F32)
    share = 1.0 / jnp.maximum(jnp.sum(assign_f, axis=1, keepdims=True), 1.0)
    assign = assign_f.astype(BF16)
    x = member_rows(in_ref, m)[:, 0:var_count]

    def embed(c, e_ref):
        cols = pl.ds(pl.multiple_of(c * chunk, chunk), chunk)
        raw = 0.5 * jnp.dot(x, w_ref[:, cols], preferred_element_type=F32)
        e_ref[...] = (raw + raw * jnp.tanh(raw)).astype(BF16)

    def pool(c, e_ref):
        cols = pl.ds(pl.multiple_of(c * chunk, chunk), chunk)
        pooled_ref[:, cols] = jnp.dot(assign, e_ref[...], preferred_element_type=F32)

    chunks = width // chunk
    embed(0, ea_ref)
    for c in range(chunks):
        here, there = (ea_ref, eb_ref) if c % 2 == 0 else (eb_ref, ea_ref)
        if c + 1 < chunks:
            embed(c + 1, there)
        pool(c, here)
    step = 32
    for out_ref, first in ((lo_ref, 0), (hi_ref, HALF_WIN)):
        for r in range(0, HALF_WIN, step):
            part = slice(first + r, first + r + step)
            pooled = pooled_ref[part, :] * share[part]
            centred = pooled - jnp.mean(pooled, axis=1, keepdims=True)
            variance = jnp.mean(centred * centred, axis=1, keepdims=True)
            out_ref[r : r + step, :] = (centred * lax.rsqrt(variance + NORM_EPS)).astype(BF16)


def qkv_kernel(halves, *refs):
    hidden_refs, (w_ref, qk_ref, vt_ref, rows_ref) = refs[:halves], refs[halves:]
    width = rows_ref.shape[1]
    half = rows_ref.shape[0] // halves
    for i, ref in enumerate(hidden_refs):
        rows_ref[i * half : (i + 1) * half, :] = ref[...]
    chunk = 256

    def project(cols):
        return jnp.dot(rows_ref[...], w_ref[:, cols], preferred_element_type=F32).astype(BF16)

    @pl.loop(0, 2 * width // chunk)
    def _(c):
        cols = pl.ds(pl.multiple_of(c * chunk, chunk), chunk)
        qk_ref[:, cols] = project(cols)

    @pl.loop(0, width // chunk)
    def _(c):
        rows = pl.ds(pl.multiple_of(c * chunk, chunk), chunk)
        vt_ref[rows, :] = project(pl.ds(pl.multiple_of(2 * width + c * chunk, chunk), chunk)).T


def attend_kernel(
    var_count, m, first_at, last_at, qk_ref, vt_ref, lo_ref, hi_ref, bef_ref, aft_ref, w_kv_ref, w_out_ref,
    w_dec_ref, *rest,
):
    if m == 0:
        out_ref, kh_ref, vth_ref, att_ref, proc_ref, left_ref, right_ref, sa_ref, sb_ref, e_ref = rest
    else:
        dec_ref, in_ref, out_ref, kh_ref, vth_ref, att_ref, proc_ref, left_ref, right_ref, sa_ref, sb_ref, e_ref = rest
    half, width = lo_ref.shape
    me = lax.axis_index("space")
    at_first, at_last = (me == first_at).astype(jnp.int32), (me == last_at).astype(jnp.int32)
    nodes = 2 * half
    head_dim = width // HEADS
    proc_ref[0:half, :] = bef_ref[...]
    proc_ref[half:, :] = aft_ref[...]
    chunk = 256

    def project(c, carry):
        cols = pl.ds(pl.multiple_of(c * chunk, chunk), chunk)
        k_src = pl.ds(pl.multiple_of(width + c * chunk, chunk), chunk)
        v_src = pl.ds(pl.multiple_of(2 * width + c * chunk, chunk), chunk)
        kh_ref[:, cols] = jnp.dot(proc_ref[...], w_kv_ref[:, k_src], preferred_element_type=F32).astype(BF16)
        vh = jnp.dot(proc_ref[...], w_kv_ref[:, v_src], preferred_element_type=F32).astype(BF16)
        vth_ref[cols, :] = vh.T
        return carry

    lax.fori_loop(0, width // chunk, project, 0)

    key_id = iota((half, 2 * half), 0)
    query_id = iota((half, 2 * half), 1)
    query_id = jnp.where(query_id >= half, query_id - half, query_id)
    big = 4 * half
    zero, low = jnp.zeros((half, 2 * half), F32), jnp.full((half, 2 * half), -1e30, F32)
    left_ref[0] = jnp.where(key_id >= query_id + at_first * big, zero, low)
    left_ref[1] = jnp.where(key_id >= query_id, zero, low)
    right_ref[0] = jnp.where(key_id <= query_id, zero, low)
    right_ref[1] = jnp.where(key_id + at_last * big <= query_id, zero, low)
    even = iota((half, LANES), 1) < head_dim
    gain = head_dim ** (-0.5) * 1.4426950408889634
    base = m * nodes

    def scores(p, s_ref):
        cols = pl.ds(pl.multiple_of(p * LANES, LANES), LANES)
        k_cols = pl.ds(pl.multiple_of(width + p * LANES, LANES), LANES)
        k_own = qk_ref[base : base + nodes, k_cols]
        for side in range(2):
            row0 = side * half
            q = qk_ref[base + row0 : base + row0 + half, cols]
            none = jnp.zeros_like(q)
            q2 = jnp.concatenate([jnp.where(even, q, none), jnp.where(even, none, q)], axis=0)
            s_all = nt_dot(jnp.concatenate([k_own, kh_ref[row0 : row0 + half, cols]], axis=0), q2)
            s_own, s_halo = s_all[0:nodes], s_all[nodes:]
            if side == 0:
                s_ref[side, 0:half] = s_own[0:half]
                s_ref[side, half:nodes] = s_own[half:] + right_ref[0]
                s_ref[side, nodes:] = s_halo + left_ref[0]
            else:
                s_ref[side, 0:half] = s_own[0:half] + left_ref[1]
                s_ref[side, half:nodes] = s_own[half:]
                s_ref[side, nodes:] = s_halo + right_ref[1]

    def finish(p, s_ref):
        cols = pl.ds(pl.multiple_of(p * LANES, LANES), LANES)
        blocks = (slice(0, half), slice(half, nodes), slice(nodes, nodes + half))
        for side in range(2):
            row0 = side * half
            s0, s1, s2 = (s_ref[side, b] for b in blocks)
            top = jnp.max(jnp.maximum(jnp.maximum(s0, s1), s2), axis=0, keepdims=True)
            total = None
            for b in blocks:
                e = jnp.exp2((s_ref[side, b] - top) * gain)
                e_ref[side, b] = e
                total = e if total is None else total + e
            inv = 1.0 / jnp.sum(total, axis=0, keepdims=True)
            p_own = (e_ref[side, 0:nodes] * inv).astype(BF16)
            p_halo = (e_ref[side, nodes:] * inv).astype(BF16)
            out = jnp.dot(vt_ref[cols, base : base + nodes], p_own, preferred_element_type=F32)
            out += jnp.dot(vth_ref[cols, row0 : row0 + half], p_halo, preferred_element_type=F32)
            pair = jnp.concatenate([out[0:head_dim, 0:half], out[head_dim:, half:]], axis=0)
            att_ref[row0 : row0 + half, cols] = pair.T.astype(BF16)

    pairs = HEADS // 2
    scores(0, sa_ref)

    def heads(i, carry):
        p = 2 * i
        scores(p + 1, sb_ref)
        finish(p, sa_ref)
        scores(jnp.minimum(p + 2, pairs - 1), sa_ref)
        finish(p + 1, sb_ref)
        return carry

    lax.fori_loop(0, pairs // 2, heads, 0)

    def mix(c, carry):
        cols = pl.ds(pl.multiple_of(c * chunk, chunk), chunk)
        mixed = jnp.dot(att_ref[...], w_out_ref[:, cols], preferred_element_type=F32)
        proc_ref[0:half, cols] = (lo_ref[:, cols].astype(F32) + mixed[0:half]).astype(BF16)
        proc_ref[half:, cols] = (hi_ref[:, cols].astype(F32) + mixed[half:]).astype(BF16)
        return carry

    lax.fori_loop(0, width // chunk, mix, 0)
    decoded = nt_dot(proc_ref[...], w_dec_ref[...]).astype(BF16)
    if m == 0:
        out_ref[...] = jnp.zeros_like(out_ref)
        out_ref[:, 0:var_count] = decoded
    else:
        n_dest = in_ref.shape[0]
        slots = n_dest * CAP
        mine_ref = att_ref.at[:, 0:LANES]
        mine_ref[...] = jnp.zeros_like(mine_ref)
        mine_ref[:, 0:var_count] = decoded
        both = jnp.concatenate([dec_ref[...], mine_ref[...]], axis=1)
        node_lane = (iota((slots, nodes), 1) + 1).astype(F32)
        asked = in_ref[:, 1].astype(F32).reshape(slots, LANES)[:, var_count : var_count + 1]
        reply = (node_lane == asked).astype(F32).astype(BF16)
        rows = jnp.dot(reply, both, preferred_element_type=F32)
        packed = [rows[:, i * LANES : (i + 1) * LANES].reshape(n_dest, 1, CAP, LANES) for i in range(2)]
        out_ref[...] = jnp.concatenate(packed, axis=1).astype(BF16)


def predict_kernel(var_count, slot_ref, back_ref, x_ref, out_ref):
    n_dest, members = back_ref.shape[:2]
    slots = n_dest * CAP
    pts = x_ref.shape[2]
    place = (iota((slots, pts), 0) == slot_ref[...]).astype(F32).astype(BF16)
    for m in range(members):
        rows = member_rows(back_ref, m)
        got = lax.dot_general(rows, place, TN, preferred_element_type=F32)
        out_ref[m] = (x_ref[m].astype(F32) + got[0:var_count]).astype(BF16)


def score_kernel(mine_ref, other_ref, target_ref, out_ref):
    fields = [r[m].astype(F32) for r in (mine_ref, other_ref) for m in range(mine_ref.shape[0])]
    count = len(fields)
    target = target_ref[...]
    skill = sum(jnp.abs(f - target) for f in fields) / count
    spread = 2.0 * sum(
        jnp.abs(fields[i] - fields[j]) for i in range(count) for j in range(i + 1, count)
    )
    fair_eps = (1.0 - FAIR_ALPHA) / count
    out_ref[...] = skill - (1.0 - fair_eps) / (2.0 * count * (count - 1)) * spread


def params(mib=32):
    return pltpu.CompilerParams(vmem_limit_bytes=mib << 20)


def cost(micros):
    return pl.CostEstimate(flops=int(micros * 7e8), bytes_accessed=1 << 20, transcendentals=0)


def on_device(
    initial_states,
    target,
    enc_owner,
    enc_local,
    dec_owner,
    dec_local,
    w_embed,
    w_qkv,
    w_out,
    w_decode,
):
    n_space = lax.axis_size("space")
    members, pts, var_count = initial_states.shape
    width = w_embed.shape[1]
    nodes, half = NODE_DEV, HALF_WIN
    slots = n_space * CAP
    in_hbm = functools.partial(pltpu.with_memory_space_constraint, memory_space=pltpu.HBM)
    rows = [in_hbm(a.reshape(1, pts)) for a in (enc_owner, enc_local, dec_owner, dec_local)]
    wire = jax.ShapeDtypeStruct((n_space, members, CAP, LANES), BF16)

    row_shape = pltpu.VMEM((1, pts), jnp.int32)
    outgoing, dec_slot, w_enc, states = pl.pallas_call(
        functools.partial(pack_kernel, var_count),
        in_specs=[HBM_SPEC] * 6,
        out_shape=(
            wire,
            jax.ShapeDtypeStruct((1, pts), jnp.int32),
            jax.ShapeDtypeStruct(w_embed.shape, BF16),
            jax.ShapeDtypeStruct((members, var_count, pts), BF16),
        ),
        scratch_shapes=[pltpu.VMEM((var_count, members, pts), BF16)]
        + [row_shape] * 4
        + [pltpu.VMEM((LANES, pts), F32), pltpu.SemaphoreType.DMA((6,))],
        compiler_params=params(),
        cost_estimate=cost(2),
        name="pack",
    )(in_hbm(jnp.transpose(initial_states, (2, 0, 1))), *rows, in_hbm(w_embed))
    at = [path_place(b) for b in range(n_space)]
    arrived = lax.all_to_all(outgoing, "space", 0, 0, tiled=True)

    half_shape = jax.ShapeDtypeStruct((half, width), BF16)
    up = [(at[i], at[(i + 1) % n_space]) for i in range(n_space)]
    down = [(j, i) for i, j in up]
    hidden, halos = [], []
    for m in range(members):
        lo, hi = pl.pallas_call(
            functools.partial(encode_kernel, var_count, m),
            out_shape=(half_shape, half_shape),
            scratch_shapes=[pltpu.VMEM((nodes, width), F32)] + [pltpu.VMEM((slots, 256), BF16)] * 2,
            compiler_params=params(),
            cost_estimate=cost(3),
            name=f"encode{m}",
        )(arrived, w_enc)
        hidden += [lo, hi]
        halos.append((lax.ppermute(hi, "space", up), lax.ppermute(lo, "space", down)))

    qk, vt = pl.pallas_call(
        functools.partial(qkv_kernel, len(hidden)),
        out_shape=(
            jax.ShapeDtypeStruct((members * nodes, 2 * width), BF16),
            jax.ShapeDtypeStruct((width, members * nodes), BF16),
        ),
        scratch_shapes=[pltpu.VMEM((members * nodes, width), BF16)],
        cost_estimate=cost(5),
        compiler_params=params(),
        name="qkv",
    )(*hidden, w_qkv)

    decoded = None
    for m in range(members):
        extra = () if m == 0 else (decoded, arrived)
        decoded = pl.pallas_call(
            functools.partial(attend_kernel, var_count, m, at[0], at[-1]),
            out_shape=jax.ShapeDtypeStruct((nodes, LANES), BF16) if m == 0 else wire,
            scratch_shapes=[
                pltpu.VMEM((nodes, width), BF16),
                pltpu.VMEM((width, nodes), BF16),
                pltpu.VMEM((nodes, width), BF16),
                pltpu.VMEM((nodes, width), BF16),
                pltpu.VMEM((2, half, nodes), F32),
                pltpu.VMEM((2, half, nodes), F32),
                pltpu.VMEM((2, nodes + half, nodes), F32),
                pltpu.VMEM((2, nodes + half, nodes), F32),
                pltpu.VMEM((2, nodes + half, nodes), F32),
            ],
            compiler_params=params(),
            cost_estimate=cost(8),
            name=f"attend{m}",
        )(qk, vt, *hidden[2 * m : 2 * m + 2], *halos[m], w_qkv, w_out, w_decode.T, *extra)
    replies = decoded

    returned = lax.all_to_all(replies, "space", 0, 0, tiled=True)
    predicted = pl.pallas_call(
        functools.partial(predict_kernel, var_count),
        out_shape=jax.ShapeDtypeStruct((members, var_count, pts), BF16),
        compiler_params=params(),
        name="predict",
    )(dec_slot, returned, states)
    other = lax.ppermute(predicted, "member", [(0, 1), (1, 0)])
    error = pl.pallas_call(
        score_kernel,
        out_shape=jax.ShapeDtypeStruct((var_count, pts), F32),
        compiler_params=params(),
        name="score",
    )(predicted, other, target.T)
    return jnp.transpose(predicted, (0, 2, 1)), error.T


def solution(mesh):
    in_specs = (
        P("member", "space", None),
        P("space", None),
        P("space", None),
        P("space", None),
        P("space", None),
        P("space", None),
        P(),
        P(),
        P(),
        P(),
    )
    out_specs = (P("member", "space", None), P("space", None))
    return jax.shard_map(
        on_device, mesh=mesh, in_specs=in_specs, out_specs=out_specs, check_vma=False
    )
```

```python
import functools

import jax
import jax.numpy as jnp
from jax import lax
from jax.experimental import pallas as pl
from jax.experimental.pallas import tpu as pltpu
from jax.sharding import PartitionSpec as P

HEADS = 16
HALF_WIN = 128
NODE_DEV = 256
CAP = 8
LANES = 128
GRID = (4, 4, 8)
Y_BITS, Z_BITS = 2, 3

FAIR_ALPHA = 0.95
NORM_EPS = 1e-05

F32 = jnp.float32
BF16 = jnp.bfloat16
NT = (((1,), (1,)), ((), ()))
TN = (((0,), (0,)), ((), ()))
VMEM_SPEC = pl.BlockSpec(memory_space=pltpu.VMEM)
HBM_SPEC = pl.BlockSpec(memory_space=pltpu.HBM)


def nt_dot(a, b):
    return lax.dot_general(a, b, NT, preferred_element_type=F32)


def iota(shape, dim):
    return lax.broadcasted_iota(jnp.int32, shape, dim)


def path_place(block):
    _, ny, nz = GRID
    line, z = block >> Z_BITS, block & (nz - 1)
    x, y = line >> Y_BITS, line & (ny - 1)
    z = z + (line & 1) * (nz - 1 - 2 * z)
    y = y + (x & 1) * (ny - 1 - 2 * y)
    return (((x << Y_BITS) + y) << Z_BITS) + z


def slot_row(owner_row):
    pts = owner_row.shape[1]
    owner = owner_row.astype(F32)
    owner_col = jnp.broadcast_to(owner, (8, pts)).T[:, 0:1]
    block = LANES
    ahead = iota((block, block), 0) < iota((block, block), 1)
    ranks = []
    for c in range(0, pts, block):
        wide = jnp.broadcast_to(owner[:, c : c + block], (block, block))
        count = jnp.where(ahead & (owner_col[c : c + block] == wide), 1.0, 0.0)
        for r in range(0, c, block):
            count += jnp.where(owner_col[r : r + block] == wide, 1.0, 0.0)
        ranks.append(jnp.sum(count, axis=0, keepdims=True))
    rank = jnp.concatenate(ranks, axis=1).astype(jnp.int32)
    return path_place(owner_row) * CAP + rank


def pack_kernel(
    var_count, x_hbm, eo_hbm, el_hbm, do_hbm, dl_hbm, w_hbm, out_ref, slot_ref, w_ref, states_ref,
    x_ref, eo_ref, el_ref, do_ref, dl_ref, aug_ref, sems,
):
    members, _, pts = states_ref.shape
    n_dest = out_ref.shape[0]
    slots = n_dest * CAP
    copies = [
        pltpu.make_async_copy(src, dst, sems.at[i])
        for i, (src, dst) in enumerate(
            [(eo_hbm, eo_ref), (do_hbm, do_ref), (el_hbm, el_ref), (dl_hbm, dl_ref), (x_hbm, x_ref), (w_hbm, w_ref)]
        )
    ]
    for copy in copies:
        copy.start()
    copies[0].wait()
    enc_slot = slot_row(eo_ref[...])
    copies[1].wait()
    dec_slot = slot_row(do_ref[...])
    slot_ref[...] = dec_slot
    slot_id = iota((slots, pts), 0)
    place = (slot_id == enc_slot).astype(F32).astype(BF16)
    request = (slot_id == dec_slot).astype(F32).astype(BF16)
    row_id = iota((LANES, pts), 0)
    copies[2].wait()
    copies[3].wait()
    enc_meta = jnp.where(row_id == var_count, el_ref[...] + 1, 0).astype(F32)
    dec_meta = jnp.where(row_id == var_count, dl_ref[...] + 1, 0).astype(F32)
    asked = nt_dot(request, dec_meta.astype(BF16))
    packed = []
    copies[4].wait()
    for m in range(members):
        aug_ref[...] = enc_meta if m == 0 else jnp.zeros_like(enc_meta)
        field = x_ref[:, m, :]
        aug_ref[0:var_count, :] = field.astype(F32)
        states_ref[m] = field
        rows = nt_dot(place, aug_ref[...].astype(BF16))
        if m == 1:
            rows = rows + asked
        packed.append(rows.reshape(n_dest, 1, CAP, LANES))
    out_ref[...] = jnp.concatenate(packed, axis=1).astype(BF16)
    copies[5].wait()


def member_rows(ref, m):
    n_dest = ref.shape[0]
    return ref[:, m].astype(F32).reshape(n_dest * CAP, LANES).astype(BF16)


def encode_kernel(var_count, m, in_ref, w_ref, lo_ref, hi_ref, pooled_ref, ea_ref, eb_ref):
    n_dest = in_ref.shape[0]
    slots = n_dest * CAP
    width = w_ref.shape[1]
    nodes = NODE_DEV
    chunk = 256
    lane_id = iota((8, LANES), 1)
    pick = (lane_id == var_count).astype(F32).astype(BF16)
    node_row = nt_dot(pick, member_rows(in_ref, 0))[0:1, :]
    node_id = (iota((nodes, slots), 0) + 1).astype(F32)
    assign_f = (node_id == node_row).astype(F32)
    share = 1.0 / jnp.maximum(jnp.sum(assign_f, axis=1, keepdims=True), 1.0)
    assign = assign_f.astype(BF16)
    x = member_rows(in_ref, m)[:, 0:var_count]

    def embed(c, e_ref):
        cols = pl.ds(pl.multiple_of(c * chunk, chunk), chunk)
        raw = 0.5 * jnp.dot(x, w_ref[:, cols], preferred_element_type=F32)
        e_ref[...] = (raw + raw * jnp.tanh(raw)).astype(BF16)

    def pool(c, e_ref):
        cols = pl.ds(pl.multiple_of(c * chunk, chunk), chunk)
        pooled_ref[:, cols] = jnp.dot(assign, e_ref[...], preferred_element_type=F32)

    chunks = width // chunk
    embed(0, ea_ref)
    for c in range(chunks):
        here, there = (ea_ref, eb_ref) if c % 2 == 0 else (eb_ref, ea_ref)
        if c + 1 < chunks:
            embed(c + 1, there)
        pool(c, here)
    step = 32
    for out_ref, first in ((lo_ref, 0), (hi_ref, HALF_WIN)):
        for r in range(0, HALF_WIN, step):
            part = slice(first + r, first + r + step)
            pooled = pooled_ref[part, :] * share[part]
            centred = pooled - jnp.mean(pooled, axis=1, keepdims=True)
            variance = jnp.mean(centred * centred, axis=1, keepdims=True)
            out_ref[r : r + step, :] = (centred * lax.rsqrt(variance + NORM_EPS)).astype(BF16)


def qkv_kernel(halves, *refs):
    hidden_refs, (w_ref, qk_ref, vt_ref, rows_ref) = refs[:halves], refs[halves:]
    width = rows_ref.shape[1]
    half = rows_ref.shape[0] // halves
    for i, ref in enumerate(hidden_refs):
        rows_ref[i * half : (i + 1) * half, :] = ref[...]

    def project(cols):
        return jnp.dot(rows_ref[...], w_ref[:, cols], preferred_element_type=F32).astype(BF16)

    chunk = 512
    for c in range(0, 2 * width, chunk):
        qk_ref[:, c : c + chunk] = project(slice(c, c + chunk))
    for c in range(0, width, chunk):
        vt_ref[c : c + chunk, :] = project(slice(2 * width + c, 2 * width + c + chunk)).T


def attend_kernel(
    var_count, m, first_at, last_at, qk_ref, vt_ref, lo_ref, hi_ref, bef_ref, aft_ref, w_kv_ref, w_out_ref,
    w_dec_ref, *rest,
):
    if m == 0:
        out_ref, kh_ref, vth_ref, att_ref, proc_ref, left_ref, right_ref, sa_ref, sb_ref, e_ref = rest
    else:
        dec_ref, in_ref, out_ref, kh_ref, vth_ref, att_ref, proc_ref, left_ref, right_ref, sa_ref, sb_ref, e_ref = rest
    half, width = lo_ref.shape
    me = lax.axis_index("space")
    at_first, at_last = (me == first_at).astype(jnp.int32), (me == last_at).astype(jnp.int32)
    nodes = 2 * half
    head_dim = width // HEADS
    proc_ref[0:half, :] = bef_ref[...]
    proc_ref[half:, :] = aft_ref[...]
    chunk = 256

    for c in range(0, width, chunk):
        k_src, v_src = slice(width + c, width + c + chunk), slice(2 * width + c, 2 * width + c + chunk)
        kh = jnp.dot(proc_ref[...], w_kv_ref[:, k_src], preferred_element_type=F32)
        kh_ref[:, c : c + chunk] = kh.astype(BF16)
        vh = jnp.dot(proc_ref[...], w_kv_ref[:, v_src], preferred_element_type=F32)
        vth_ref[c : c + chunk, :] = vh.astype(BF16).T

    key_id = iota((half, 2 * half), 0)
    query_id = iota((half, 2 * half), 1)
    query_id = jnp.where(query_id >= half, query_id - half, query_id)
    big = 4 * half
    zero, low = jnp.zeros((half, 2 * half), F32), jnp.full((half, 2 * half), -1e30, F32)
    left_ref[0] = jnp.where(key_id >= query_id + at_first * big, zero, low)
    left_ref[1] = jnp.where(key_id >= query_id, zero, low)
    right_ref[0] = jnp.where(key_id <= query_id, zero, low)
    right_ref[1] = jnp.where(key_id + at_last * big <= query_id, zero, low)
    even = iota((half, LANES), 1) < head_dim
    gain = head_dim ** (-0.5) * 1.4426950408889634
    base = m * nodes

    def scores(p, s_ref):
        cols = slice(p * LANES, (p + 1) * LANES)
        k_cols = slice(width + p * LANES, width + (p + 1) * LANES)
        k_own = qk_ref[base : base + nodes, k_cols]
        for side in range(2):
            row0 = side * half
            q = qk_ref[base + row0 : base + row0 + half, cols]
            none = jnp.zeros_like(q)
            q2 = jnp.concatenate([jnp.where(even, q, none), jnp.where(even, none, q)], axis=0)
            s_all = nt_dot(jnp.concatenate([k_own, kh_ref[row0 : row0 + half, cols]], axis=0), q2)
            s_own, s_halo = s_all[0:nodes], s_all[nodes:]
            if side == 0:
                s_ref[side, 0:half] = s_own[0:half]
                s_ref[side, half:nodes] = s_own[half:] + right_ref[0]
                s_ref[side, nodes:] = s_halo + left_ref[0]
            else:
                s_ref[side, 0:half] = s_own[0:half] + left_ref[1]
                s_ref[side, half:nodes] = s_own[half:]
                s_ref[side, nodes:] = s_halo + right_ref[1]

    def finish(p, s_ref):
        cols = slice(p * LANES, (p + 1) * LANES)
        blocks = (slice(0, half), slice(half, nodes), slice(nodes, nodes + half))
        for side in range(2):
            row0 = side * half
            s0, s1, s2 = (s_ref[side, b] for b in blocks)
            top = jnp.max(jnp.maximum(jnp.maximum(s0, s1), s2), axis=0, keepdims=True)
            total = None
            for b in blocks:
                e = jnp.exp2((s_ref[side, b] - top) * gain)
                e_ref[side, b] = e
                total = e if total is None else total + e
            inv = 1.0 / jnp.sum(total, axis=0, keepdims=True)
            p_own = (e_ref[side, 0:nodes] * inv).astype(BF16)
            p_halo = (e_ref[side, nodes:] * inv).astype(BF16)
            out = jnp.dot(vt_ref[cols, base : base + nodes], p_own, preferred_element_type=F32)
            out += jnp.dot(vth_ref[cols, row0 : row0 + half], p_halo, preferred_element_type=F32)
            pair = jnp.concatenate([out[0:head_dim, 0:half], out[head_dim:, half:]], axis=0)
            att_ref[row0 : row0 + half, cols] = pair.T.astype(BF16)

    pairs = HEADS // 2
    scores(0, sa_ref)

    for p in range(pairs):
        here, there = (sa_ref, sb_ref) if p % 2 == 0 else (sb_ref, sa_ref)
        if p + 1 < pairs:
            scores(p + 1, there)
        finish(p, here)

    for c in range(0, width, chunk):
        cols = slice(c, c + chunk)
        mixed = jnp.dot(att_ref[...], w_out_ref[:, cols], preferred_element_type=F32)
        proc_ref[0:half, cols] = (lo_ref[:, cols].astype(F32) + mixed[0:half]).astype(BF16)
        proc_ref[half:, cols] = (hi_ref[:, cols].astype(F32) + mixed[half:]).astype(BF16)
    decoded = nt_dot(proc_ref[...], w_dec_ref[...]).astype(BF16)
    if m == 0:
        out_ref[...] = jnp.zeros_like(out_ref)
        out_ref[:, 0:var_count] = decoded
    else:
        n_dest = in_ref.shape[0]
        slots = n_dest * CAP
        mine_ref = att_ref.at[:, 0:LANES]
        mine_ref[...] = jnp.zeros_like(mine_ref)
        mine_ref[:, 0:var_count] = decoded
        both = jnp.concatenate([dec_ref[...], mine_ref[...]], axis=1)
        node_lane = (iota((slots, nodes), 1) + 1).astype(F32)
        asked = in_ref[:, 1].astype(F32).reshape(slots, LANES)[:, var_count : var_count + 1]
        reply = (node_lane == asked).astype(F32).astype(BF16)
        rows = jnp.dot(reply, both, preferred_element_type=F32)
        packed = [rows[:, i * LANES : (i + 1) * LANES].reshape(n_dest, 1, CAP, LANES) for i in range(2)]
        out_ref[...] = jnp.concatenate(packed, axis=1).astype(BF16)


def predict_kernel(var_count, slot_ref, back_ref, x_ref, out_ref):
    n_dest, members = back_ref.shape[:2]
    slots = n_dest * CAP
    pts = x_ref.shape[2]
    place = (iota((slots, pts), 0) == slot_ref[...]).astype(F32).astype(BF16)
    for m in range(members):
        rows = member_rows(back_ref, m)
        got = lax.dot_general(rows, place, TN, preferred_element_type=F32)
        out_ref[m] = (x_ref[m].astype(F32) + got[0:var_count]).astype(BF16)


def score_kernel(mine_ref, other_ref, target_ref, out_ref):
    fields = [r[m].astype(F32) for r in (mine_ref, other_ref) for m in range(mine_ref.shape[0])]
    count = len(fields)
    target = target_ref[...]
    skill = sum(jnp.abs(f - target) for f in fields) / count
    spread = 2.0 * sum(
        jnp.abs(fields[i] - fields[j]) for i in range(count) for j in range(i + 1, count)
    )
    fair_eps = (1.0 - FAIR_ALPHA) / count
    out_ref[...] = skill - (1.0 - fair_eps) / (2.0 * count * (count - 1)) * spread


def params(mib=32):
    return pltpu.CompilerParams(vmem_limit_bytes=mib << 20)


def cost(micros):
    return pl.CostEstimate(flops=int(micros * 7e8), bytes_accessed=1 << 20, transcendentals=0)


def on_device(
    initial_states,
    target,
    enc_owner,
    enc_local,
    dec_owner,
    dec_local,
    w_embed,
    w_qkv,
    w_out,
    w_decode,
):
    n_space = lax.axis_size("space")
    members, pts, var_count = initial_states.shape
    width = w_embed.shape[1]
    nodes, half = NODE_DEV, HALF_WIN
    slots = n_space * CAP
    in_hbm = functools.partial(pltpu.with_memory_space_constraint, memory_space=pltpu.HBM)
    rows = [in_hbm(a.reshape(1, pts)) for a in (enc_owner, enc_local, dec_owner, dec_local)]
    wire = jax.ShapeDtypeStruct((n_space, members, CAP, LANES), BF16)

    row_shape = pltpu.VMEM((1, pts), jnp.int32)
    outgoing, dec_slot, w_enc, states = pl.pallas_call(
        functools.partial(pack_kernel, var_count),
        in_specs=[HBM_SPEC] * 6,
        out_shape=(
            wire,
            jax.ShapeDtypeStruct((1, pts), jnp.int32),
            jax.ShapeDtypeStruct(w_embed.shape, BF16),
            jax.ShapeDtypeStruct((members, var_count, pts), BF16),
        ),
        scratch_shapes=[pltpu.VMEM((var_count, members, pts), BF16)]
        + [row_shape] * 4
        + [pltpu.VMEM((LANES, pts), F32), pltpu.SemaphoreType.DMA((6,))],
        compiler_params=params(),
        cost_estimate=cost(2),
        name="pack",
    )(in_hbm(jnp.transpose(initial_states, (2, 0, 1))), *rows, in_hbm(w_embed))
    at = [path_place(b) for b in range(n_space)]
    arrived = lax.all_to_all(outgoing, "space", 0, 0, tiled=True)

    half_shape = jax.ShapeDtypeStruct((half, width), BF16)
    up = [(at[i], at[(i + 1) % n_space]) for i in range(n_space)]
    down = [(j, i) for i, j in up]
    hidden, halos = [], []
    for m in range(members):
        lo, hi = pl.pallas_call(
            functools.partial(encode_kernel, var_count, m),
            out_shape=(half_shape, half_shape),
            scratch_shapes=[pltpu.VMEM((nodes, width), F32)] + [pltpu.VMEM((slots, 256), BF16)] * 2,
            compiler_params=params(),
            cost_estimate=cost(3),
            name=f"encode{m}",
        )(arrived, w_enc)
        hidden += [lo, hi]
        halos.append((lax.ppermute(hi, "space", up), lax.ppermute(lo, "space", down)))

    qk, vt = pl.pallas_call(
        functools.partial(qkv_kernel, len(hidden)),
        out_shape=(
            jax.ShapeDtypeStruct((members * nodes, 2 * width), BF16),
            jax.ShapeDtypeStruct((width, members * nodes), BF16),
        ),
        scratch_shapes=[pltpu.VMEM((members * nodes, width), BF16)],
        cost_estimate=cost(5),
        compiler_params=params(),
        name="qkv",
    )(*hidden, w_qkv)

    decoded = None
    for m in range(members):
        extra = () if m == 0 else (decoded, arrived)
        decoded = pl.pallas_call(
            functools.partial(attend_kernel, var_count, m, at[0], at[-1]),
            out_shape=jax.ShapeDtypeStruct((nodes, LANES), BF16) if m == 0 else wire,
            scratch_shapes=[
                pltpu.VMEM((nodes, width), BF16),
                pltpu.VMEM((width, nodes), BF16),
                pltpu.VMEM((nodes, width), BF16),
                pltpu.VMEM((nodes, width), BF16),
                pltpu.VMEM((2, half, nodes), F32),
                pltpu.VMEM((2, half, nodes), F32),
                pltpu.VMEM((2, nodes + half, nodes), F32),
                pltpu.VMEM((2, nodes + half, nodes), F32),
                pltpu.VMEM((2, nodes + half, nodes), F32),
            ],
            compiler_params=params(),
            cost_estimate=cost(8),
            name=f"attend{m}",
        )(qk, vt, *hidden[2 * m : 2 * m + 2], *halos[m], w_qkv, w_out, w_decode.T, *extra)
    replies = decoded

    returned = lax.all_to_all(replies, "space", 0, 0, tiled=True)
    predicted = pl.pallas_call(
        functools.partial(predict_kernel, var_count),
        out_shape=jax.ShapeDtypeStruct((members, var_count, pts), BF16),
        compiler_params=params(),
        name="predict",
    )(dec_slot, returned, states)
    other = lax.ppermute(predicted, "member", [(0, 1), (1, 0)])
    error = pl.pallas_call(
        score_kernel,
        out_shape=jax.ShapeDtypeStruct((var_count, pts), F32),
        compiler_params=params(),
        name="score",
    )(predicted, other, target.T)
    return jnp.transpose(predicted, (0, 2, 1)), error.T


def solution(mesh):
    in_specs = (
        P("member", "space", None),
        P("space", None),
        P("space", None),
        P("space", None),
        P("space", None),
        P("space", None),
        P(),
        P(),
        P(),
        P(),
    )
    out_specs = (P("member", "space", None), P("space", None))
    return jax.shard_map(
        on_device, mesh=mesh, in_specs=in_specs, out_specs=out_specs, check_vma=False
    )
```

```python
import functools

import jax
import jax.numpy as jnp
from jax import lax
from jax.experimental import pallas as pl
from jax.experimental.pallas import tpu as pltpu
from jax.sharding import PartitionSpec as P

HEADS = 16
HALF_WIN = 128
NODE_DEV = 256
CAP = 8
CAP_BITS = 3
META = 104
LANES = 128
GRID = (4, 4, 8)
Y_BITS, Z_BITS = 2, 3

FAIR_ALPHA = 0.95
NORM_EPS = 1e-05

F32 = jnp.float32
BF16 = jnp.bfloat16
NT = (((1,), (1,)), ((), ()))
TN = (((0,), (0,)), ((), ()))
VMEM_SPEC = pl.BlockSpec(memory_space=pltpu.VMEM)
HBM_SPEC = pl.BlockSpec(memory_space=pltpu.HBM)


def nt_dot(a, b):
    return lax.dot_general(a, b, NT, preferred_element_type=F32)


def iota(shape, dim):
    return lax.broadcasted_iota(jnp.int32, shape, dim)


def path_place(block):
    _, ny, nz = GRID
    line, z = block >> Z_BITS, block & (nz - 1)
    x, y = line >> Y_BITS, line & (ny - 1)
    z = z + (line & 1) * (nz - 1 - 2 * z)
    y = y + (x & 1) * (ny - 1 - 2 * y)
    return (((x << Y_BITS) + y) << Z_BITS) + z


def slot_row(owner_row):
    pts = owner_row.shape[1]
    owner = owner_row.astype(F32)
    owner_col = jnp.broadcast_to(owner, (8, pts)).T[:, 0:1]
    block = LANES
    ahead = iota((block, block), 0) < iota((block, block), 1)
    ranks = []
    for c in range(0, pts, block):
        wide = jnp.broadcast_to(owner[:, c : c + block], (block, block))
        count = jnp.where(ahead & (owner_col[c : c + block] == wide), 1.0, 0.0)
        for r in range(0, c, block):
            count += jnp.where(owner_col[r : r + block] == wide, 1.0, 0.0)
        ranks.append(jnp.sum(count, axis=0, keepdims=True))
    rank = jnp.concatenate(ranks, axis=1).astype(jnp.int32)
    return path_place(owner_row) * CAP + rank


def one_hot(count, row):
    ids = iota((count, row.shape[1]), 0).astype(jnp.int16)
    return jnp.where(ids == row.astype(jnp.int16), jnp.ones((), BF16), jnp.zeros((), BF16))


def pack_kernel(
    var_count, x_hbm, eo_hbm, el_hbm, do_hbm, dl_hbm, w_hbm, out_ref, slot_ref, w_ref, states_ref,
    x_ref, eo_ref, el_ref, do_ref, dl_ref, sems,
):
    members, _, pts = states_ref.shape
    n_dest = out_ref.shape[0]
    slots = n_dest * CAP
    pairs = [
        (eo_hbm, eo_ref),
        (do_hbm, do_ref),
        (el_hbm, el_ref),
        (dl_hbm, dl_ref),
        (x_hbm, x_ref),
        (w_hbm, w_ref),
    ]
    copies = [pltpu.make_async_copy(src, dst, sems.at[i]) for i, (src, dst) in enumerate(pairs)]
    for copy in copies:
        copy.start()
    copies[0].wait()
    enc_slot = slot_row(eo_ref[...])
    copies[1].wait()
    dec_slot = slot_row(do_ref[...])
    slot_ref[...] = dec_slot
    copies[2].wait()
    copies[3].wait()
    copies[4].wait()
    rows_in = members * var_count
    lanes = members * LANES
    row_id, col_id = iota((lanes, rows_in), 0), iota((lanes, rows_in), 1)
    var, m = row_id & (LANES - 1), row_id >> 7
    apart = ((var * members + m == col_id) & (var < var_count)).astype(F32).astype(BF16)
    fields = jnp.dot(apart, x_ref[...].reshape(rows_in, pts), preferred_element_type=F32)
    for i in range(members):
        states_ref[i] = fields[i * LANES : i * LANES + var_count].astype(BF16)
    line_id = iota((lanes, pts), 0)
    fields += jnp.where(line_id == var_count, el_ref[...] + 1, 0).astype(F32)
    rows = nt_dot(one_hot(slots, enc_slot), fields.astype(BF16)).reshape(n_dest, CAP, lanes)
    rank = (dec_slot & (CAP - 1)) + META
    requests = jnp.where(iota((LANES, pts), 0) == rank, dl_ref[...] + 1, 0).astype(F32)
    asked = nt_dot(one_hot(n_dest, dec_slot >> CAP_BITS), requests.astype(BF16))
    top = iota((n_dest, CAP, LANES), 1) == 0
    asked = jnp.where(top, jnp.broadcast_to(asked[:, None, :], (n_dest, CAP, LANES)), 0.0)
    out_ref[:, :, 0:LANES] = rows[:, :, 0:LANES].astype(BF16)
    out_ref[:, :, LANES:] = (rows[:, :, LANES:] + asked).astype(BF16)
    copies[5].wait()
    w_ref[...] = w_ref[...] * jnp.asarray(0.5, BF16)


def encode_kernel(var_count, m, in_ref, w_ref, lo_ref, hi_ref, pooled_ref, ea_ref, eb_ref):
    n_dest = in_ref.shape[0]
    slots = n_dest * CAP
    width = w_ref.shape[1]
    nodes = NODE_DEV
    chunk = 256
    arrived = in_ref[...].reshape(slots, in_ref.shape[2])
    lane_id = iota((8, LANES), 1)
    pick = (lane_id == var_count).astype(F32).astype(BF16)
    node_row = nt_dot(pick, arrived[:, 0:LANES])[0:1, :]
    assign = one_hot(nodes, node_row.astype(jnp.int32) - 1)
    share = 1.0 / jnp.maximum(jnp.sum(assign.astype(F32), axis=1, keepdims=True), 1.0)
    x = arrived[:, m * LANES : m * LANES + var_count]

    def embed(c, e_ref):
        cols = pl.ds(pl.multiple_of(c * chunk, chunk), chunk)
        raw = jnp.dot(x, w_ref[:, cols], preferred_element_type=F32)
        e_ref[...] = (raw + raw * jnp.tanh(raw)).astype(BF16)

    def pool(c, e_ref):
        cols = pl.ds(pl.multiple_of(c * chunk, chunk), chunk)
        pooled_ref[:, cols] = jnp.dot(assign, e_ref[...], preferred_element_type=F32)

    chunks = width // chunk
    embed(0, ea_ref)
    for c in range(chunks):
        here, there = (ea_ref, eb_ref) if c % 2 == 0 else (eb_ref, ea_ref)
        if c + 1 < chunks:
            embed(c + 1, there)
        pool(c, here)
    step = 32
    for out_ref, first in ((lo_ref, 0), (hi_ref, HALF_WIN)):
        for r in range(0, HALF_WIN, step):
            part = slice(first + r, first + r + step)
            pooled = pooled_ref[part, :] * share[part]
            centred = pooled - jnp.mean(pooled, axis=1, keepdims=True)
            variance = jnp.mean(centred * centred, axis=1, keepdims=True)
            out_ref[r : r + step, :] = (centred * lax.rsqrt(variance + NORM_EPS)).astype(BF16)


def qkv_kernel(halves, *refs):
    hidden_refs, (w_ref, qk_ref, vt_ref, rows_ref) = refs[:halves], refs[halves:]
    width = rows_ref.shape[1]
    half = rows_ref.shape[0] // halves
    for i, ref in enumerate(hidden_refs):
        rows_ref[i * half : (i + 1) * half, :] = ref[...]

    def project(cols):
        return jnp.dot(rows_ref[...], w_ref[:, cols], preferred_element_type=F32).astype(BF16)

    chunk = 512
    for c in range(0, 2 * width, chunk):
        qk_ref[:, c : c + chunk] = project(slice(c, c + chunk))
    for c in range(0, width, chunk):
        vt_ref[c : c + chunk, :] = project(slice(2 * width + c, 2 * width + c + chunk)).T


def attend_kernel(
    var_count, m, first_at, last_at, qk_ref, vt_ref, lo_ref, hi_ref, bef_ref, aft_ref, w_kv_ref, w_out_ref,
    w_dec_ref, *rest,
):
    if m == 0:
        out_ref, kh_ref, vth_ref, att_ref, proc_ref, left_ref, right_ref, sa_ref, sb_ref, e_ref, halo_ref = rest
    else:
        dec_ref, in_ref, out_ref, kh_ref, vth_ref, att_ref, proc_ref, left_ref, right_ref, sa_ref, sb_ref, e_ref, halo_ref, reply_ref = rest
    half, width = lo_ref.shape
    me = lax.axis_index("space")
    at_first, at_last = (me == first_at).astype(jnp.int32), (me == last_at).astype(jnp.int32)
    nodes = 2 * half
    head_dim = width // HEADS
    halo_ref[0:half, :] = bef_ref[...]
    halo_ref[half:, :] = aft_ref[...]
    chunk = 256

    def project(c):
        k_src, v_src = slice(width + c, width + c + chunk), slice(2 * width + c, 2 * width + c + chunk)
        kh = jnp.dot(halo_ref[...], w_kv_ref[:, k_src], preferred_element_type=F32)
        kh_ref[:, c : c + chunk] = kh.astype(BF16)
        vh = jnp.dot(halo_ref[...], w_kv_ref[:, v_src], preferred_element_type=F32)
        vth_ref[c : c + chunk, :] = vh.astype(BF16).T

    key_id = iota((half, 2 * half), 0)
    query_id = iota((half, 2 * half), 1)
    query_id = jnp.where(query_id >= half, query_id - half, query_id)
    big = 4 * half
    zero, low = jnp.zeros((half, 2 * half), F32), jnp.full((half, 2 * half), -1e30, F32)
    left_ref[0] = jnp.where(key_id >= query_id + at_first * big, zero, low)
    left_ref[1] = jnp.where(key_id >= query_id, zero, low)
    right_ref[0] = jnp.where(key_id <= query_id, zero, low)
    right_ref[1] = jnp.where(key_id + at_last * big <= query_id, zero, low)
    even = iota((half, LANES), 1) < head_dim
    gain = head_dim ** (-0.5) * 1.4426950408889634
    base = m * nodes

    def scores(p, s_ref):
        cols = slice(p * LANES, (p + 1) * LANES)
        k_cols = slice(width + p * LANES, width + (p + 1) * LANES)
        k_own = qk_ref[base : base + nodes, k_cols]
        for side in range(2):
            row0 = side * half
            q = qk_ref[base + row0 : base + row0 + half, cols]
            none = jnp.zeros_like(q)
            q2 = jnp.concatenate([jnp.where(even, q, none), jnp.where(even, none, q)], axis=0)
            s_all = nt_dot(jnp.concatenate([k_own, kh_ref[row0 : row0 + half, cols]], axis=0), q2)
            s_own, s_halo = s_all[0:nodes], s_all[nodes:]
            if side == 0:
                s_ref[side, 0:half] = s_own[0:half]
                s_ref[side, half:nodes] = s_own[half:] + right_ref[0]
                s_ref[side, nodes:] = s_halo + left_ref[0]
            else:
                s_ref[side, 0:half] = s_own[0:half] + left_ref[1]
                s_ref[side, half:nodes] = s_own[half:]
                s_ref[side, nodes:] = s_halo + right_ref[1]

    def finish(p, s_ref):
        cols = slice(p * LANES, (p + 1) * LANES)
        blocks = (slice(0, half), slice(half, nodes), slice(nodes, nodes + half))
        for side in range(2):
            row0 = side * half
            s0, s1, s2 = (s_ref[side, b] for b in blocks)
            top = jnp.max(jnp.maximum(jnp.maximum(s0, s1), s2), axis=0, keepdims=True)
            total = None
            for b in blocks:
                e = jnp.exp2((s_ref[side, b] - top) * gain)
                e_ref[side, b] = e
                total = e if total is None else total + e
            inv = 1.0 / jnp.sum(total, axis=0, keepdims=True)
            p_own = (e_ref[side, 0:nodes] * inv).astype(BF16)
            p_halo = (e_ref[side, nodes:] * inv).astype(BF16)
            out = jnp.dot(vt_ref[cols, base : base + nodes], p_own, preferred_element_type=F32)
            out += jnp.dot(vth_ref[cols, row0 : row0 + half], p_halo, preferred_element_type=F32)
            pair = jnp.concatenate([out[0:head_dim, 0:half], out[head_dim:, half:]], axis=0)
            att_ref[row0 : row0 + half, cols] = pair.T.astype(BF16)

    if m == 1:
        n_dest = in_ref.shape[0]
        slots = n_dest * CAP
        cube = (n_dest, CAP, LANES)
        asked = in_ref[:, :, LANES:].astype(F32)
        asked = jnp.broadcast_to(asked[:, 0:1, :], cube)
        asked = jnp.where(iota(cube, 2) == iota(cube, 1) + META, asked, 0.0)
        asked = jnp.sum(asked, axis=2, keepdims=True).reshape(slots, 1)
        node_lane = (iota((slots, nodes), 1) + 1).astype(F32)
        reply_ref[...] = (node_lane == asked).astype(F32).astype(BF16)

    pairs = HEADS // 2
    per_chunk = chunk // LANES
    project(0)
    scores(0, sa_ref)
    for p in range(pairs):
        here, there = (sa_ref, sb_ref) if p % 2 == 0 else (sb_ref, sa_ref)
        if p % per_chunk == 0 and p + per_chunk < pairs:
            project((p // per_chunk + 1) * chunk)
        if p + 1 < pairs:
            scores(p + 1, there)
        finish(p, here)

    for c in range(0, width, chunk):
        cols = slice(c, c + chunk)
        mixed = jnp.dot(att_ref[...], w_out_ref[:, cols], preferred_element_type=F32)
        proc_ref[0:half, cols] = (lo_ref[:, cols].astype(F32) + mixed[0:half]).astype(BF16)
        proc_ref[half:, cols] = (hi_ref[:, cols].astype(F32) + mixed[half:]).astype(BF16)
    decoded = nt_dot(proc_ref[...], w_dec_ref[...]).astype(BF16)
    if m == 0:
        out_ref[...] = jnp.zeros_like(out_ref)
        out_ref[:, 0:var_count] = decoded
    else:
        mine_ref = att_ref.at[:, 0:LANES]
        mine_ref[...] = jnp.zeros_like(mine_ref)
        mine_ref[:, 0:var_count] = decoded
        both = jnp.concatenate([dec_ref[...], mine_ref[...]], axis=1)
        reply = reply_ref[...]
        rows = jnp.dot(reply, both, preferred_element_type=F32).astype(BF16)
        out_ref[...] = rows.reshape(out_ref.shape)


def predict_kernel(var_count, slot_ref, back_ref, x_ref, out_ref):
    n_dest, _, lanes = back_ref.shape
    place = one_hot(n_dest * CAP, slot_ref[...])
    rows = back_ref[...].reshape(n_dest * CAP, lanes)
    got = lax.dot_general(rows, place, TN, preferred_element_type=F32)
    for m in range(x_ref.shape[0]):
        out_ref[m] = (x_ref[m].astype(F32) + got[m * LANES : m * LANES + var_count]).astype(BF16)


def score_kernel(mine_ref, other_ref, target_ref, out_ref):
    fields = [r[m].astype(F32) for r in (mine_ref, other_ref) for m in range(mine_ref.shape[0])]
    count = len(fields)
    target = target_ref[...]
    skill = sum(jnp.abs(f - target) for f in fields) / count
    spread = 2.0 * sum(
        jnp.abs(fields[i] - fields[j]) for i in range(count) for j in range(i + 1, count)
    )
    fair_eps = (1.0 - FAIR_ALPHA) / count
    out_ref[...] = skill - (1.0 - fair_eps) / (2.0 * count * (count - 1)) * spread


def params(mib=32):
    return pltpu.CompilerParams(vmem_limit_bytes=mib << 20)


def cost(micros):
    return pl.CostEstimate(flops=int(micros * 7e8), bytes_accessed=1 << 20, transcendentals=0)


def on_device(
    initial_states,
    target,
    enc_owner,
    enc_local,
    dec_owner,
    dec_local,
    w_embed,
    w_qkv,
    w_out,
    w_decode,
):
    n_space = lax.axis_size("space")
    members, pts, var_count = initial_states.shape
    width = w_embed.shape[1]
    nodes, half = NODE_DEV, HALF_WIN
    slots = n_space * CAP
    in_hbm = functools.partial(pltpu.with_memory_space_constraint, memory_space=pltpu.HBM)
    rows = [in_hbm(a.reshape(1, pts)) for a in (enc_owner, enc_local, dec_owner, dec_local)]
    wire = jax.ShapeDtypeStruct((n_space, CAP, members * LANES), BF16)

    row_shape = pltpu.VMEM((1, pts), jnp.int32)
    outgoing, dec_slot, w_enc, states = pl.pallas_call(
        functools.partial(pack_kernel, var_count),
        in_specs=[HBM_SPEC] * 6,
        out_shape=(
            wire,
            jax.ShapeDtypeStruct((1, pts), jnp.int32),
            jax.ShapeDtypeStruct(w_embed.shape, BF16),
            jax.ShapeDtypeStruct((members, var_count, pts), BF16),
        ),
        scratch_shapes=[pltpu.VMEM((var_count, members, pts), BF16)]
        + [row_shape] * 4
        + [pltpu.SemaphoreType.DMA((6,))],
        compiler_params=params(),
        cost_estimate=cost(2),
        name="pack",
    )(in_hbm(jnp.transpose(initial_states, (2, 0, 1))), *rows, in_hbm(w_embed))
    at = [path_place(b) for b in range(n_space)]
    arrived = lax.all_to_all(outgoing, "space", 0, 0, tiled=True)

    half_shape = jax.ShapeDtypeStruct((half, width), BF16)
    up = [(at[i], at[(i + 1) % n_space]) for i in range(n_space)]
    down = [(j, i) for i, j in up]
    hidden, halos = [], []
    for m in range(members):
        lo, hi = pl.pallas_call(
            functools.partial(encode_kernel, var_count, m),
            out_shape=(half_shape, half_shape),
            scratch_shapes=[pltpu.VMEM((nodes, width), F32)] + [pltpu.VMEM((slots, 256), BF16)] * 2,
            compiler_params=params(),
            cost_estimate=cost(3),
            name=f"encode{m}",
        )(arrived, w_enc)
        hidden += [lo, hi]
        halos.append((lax.ppermute(hi, "space", up), lax.ppermute(lo, "space", down)))

    qk, vt = pl.pallas_call(
        functools.partial(qkv_kernel, len(hidden)),
        out_shape=(
            jax.ShapeDtypeStruct((members * nodes, 2 * width), BF16),
            jax.ShapeDtypeStruct((width, members * nodes), BF16),
        ),
        scratch_shapes=[pltpu.VMEM((members * nodes, width), BF16)],
        cost_estimate=cost(5),
        compiler_params=params(),
        name="qkv",
    )(*hidden, w_qkv)

    decoded = None
    for m in range(members):
        extra = () if m == 0 else (decoded, arrived)
        decoded = pl.pallas_call(
            functools.partial(attend_kernel, var_count, m, at[0], at[-1]),
            out_shape=jax.ShapeDtypeStruct((nodes, LANES), BF16) if m == 0 else wire,
            scratch_shapes=[
                pltpu.VMEM((nodes, width), BF16),
                pltpu.VMEM((width, nodes), BF16),
                pltpu.VMEM((nodes, width), BF16),
                pltpu.VMEM((nodes, width), BF16),
                pltpu.VMEM((2, half, nodes), F32),
                pltpu.VMEM((2, half, nodes), F32),
                pltpu.VMEM((2, nodes + half, nodes), F32),
                pltpu.VMEM((2, nodes + half, nodes), F32),
                pltpu.VMEM((2, nodes + half, nodes), F32),
                pltpu.VMEM((nodes, width), BF16),
            ]
            + [pltpu.VMEM((slots, nodes), BF16)] * m,
            compiler_params=params(),
            cost_estimate=cost(8),
            name=f"attend{m}",
        )(qk, vt, *hidden[2 * m : 2 * m + 2], *halos[m], w_qkv, w_out, w_decode.T, *extra)
    replies = decoded

    returned = lax.all_to_all(replies, "space", 0, 0, tiled=True)
    predicted = pl.pallas_call(
        functools.partial(predict_kernel, var_count),
        out_shape=jax.ShapeDtypeStruct((members, var_count, pts), BF16),
        compiler_params=params(),
        name="predict",
    )(dec_slot, returned, states)
    other = lax.ppermute(predicted, "member", [(0, 1), (1, 0)])
    error = pl.pallas_call(
        score_kernel,
        out_shape=jax.ShapeDtypeStruct((var_count, pts), F32),
        compiler_params=params(),
        name="score",
    )(predicted, other, target.T)
    return jnp.transpose(predicted, (0, 2, 1)), error.T


def solution(mesh):
    in_specs = (
        P("member", "space", None),
        P("space", None),
        P("space", None),
        P("space", None),
        P("space", None),
        P("space", None),
        P(),
        P(),
        P(),
        P(),
    )
    out_specs = (P("member", "space", None), P("space", None))
    return jax.shard_map(
        on_device, mesh=mesh, in_specs=in_specs, out_specs=out_specs, check_vma=False
    )
```

```python
import functools

import jax
import jax.numpy as jnp
import numpy as np
from jax import lax
from jax.experimental import pallas as pl
from jax.experimental.pallas import tpu as pltpu
from jax.sharding import PartitionSpec as P

HEADS = 16
HALF_WIN = 128
NODE_DEV = 256
CAP = 8
CAP_BITS = 3
META = 104
LANES = 128
PATHS = (
    (
        32, 40, 72, 64, 96, 104, 112, 120, 88, 80, 48, 56, 24, 16, 8, 0,
        1, 33, 65, 97, 105, 73, 41, 49, 81, 113, 121, 89, 57, 25, 17, 9,
        10, 2, 34, 66, 98, 106, 74, 42, 50, 82, 114, 122, 90, 58, 26, 18,
        19, 51, 83, 75, 43, 11, 3, 35, 67, 99, 107, 115, 123, 91, 59, 27,
        28, 124, 100, 4, 36, 68, 76, 108, 12, 44, 52, 20, 116, 84, 92, 60,
        61, 93, 125, 29, 5, 37, 69, 101, 109, 13, 45, 77, 85, 117, 21, 53,
        54, 86, 118, 126, 94, 62, 30, 22, 14, 6, 38, 70, 102, 110, 78, 46,
        47, 79, 111, 15, 23, 55, 87, 119, 127, 31, 63, 95, 71, 103, 7, 39,
    ),
    (
        0, 7, 6, 5, 4, 3, 2, 1, 9, 8, 15, 14, 13, 12, 11, 10,
        18, 17, 16, 23, 22, 21, 20, 19, 27, 26, 25, 24, 31, 30, 29, 28,
        60, 59, 58, 57, 56, 63, 62, 61, 53, 52, 51, 50, 49, 48, 55, 54,
        46, 45, 44, 43, 42, 41, 40, 47, 39, 38, 37, 36, 35, 34, 33, 32,
        64, 71, 70, 69, 68, 67, 66, 65, 73, 72, 79, 78, 77, 76, 75, 74,
        82, 81, 80, 87, 86, 85, 84, 83, 91, 90, 89, 88, 95, 94, 93, 92,
        124, 123, 122, 121, 120, 127, 126, 125, 117, 116, 115, 114, 113, 112, 119, 118,
        110, 109, 108, 107, 106, 105, 104, 111, 103, 102, 101, 100, 99, 98, 97, 96,
    ),
)

FAIR_ALPHA = 0.95
NORM_EPS = 1e-05

F32 = jnp.float32
BF16 = jnp.bfloat16
NT = (((1,), (1,)), ((), ()))
TN = (((0,), (0,)), ((), ()))
VMEM_SPEC = pl.BlockSpec(memory_space=pltpu.VMEM)
HBM_SPEC = pl.BlockSpec(memory_space=pltpu.HBM)


def nt_dot(a, b):
    return lax.dot_general(a, b, NT, preferred_element_type=F32)


def iota(shape, dim):
    return lax.broadcasted_iota(jnp.int32, shape, dim)


def column(row):
    return jnp.broadcast_to(row, (8, row.shape[1])).T[:, 0:1]


def rank_row(owner):
    pts = owner.shape[1]
    owner_col = column(owner)
    block = LANES
    ahead = iota((block, block), 0) < iota((block, block), 1)
    ranks = []
    for c in range(0, pts, block):
        wide = jnp.broadcast_to(owner[:, c : c + block], (block, block))
        count = jnp.where(ahead & (owner_col[c : c + block] == wide), 1.0, 0.0)
        for r in range(0, c, block):
            count += jnp.where(owner_col[r : r + block] == wide, 1.0, 0.0)
        ranks.append(jnp.sum(count, axis=0, keepdims=True))
    return jnp.concatenate(ranks, axis=1)


def device_row(owner, block_of):
    shape = (block_of.shape[0], owner.shape[1])
    found = block_of == jnp.broadcast_to(owner, shape)
    return jnp.sum(jnp.where(found, iota(shape, 0).astype(F32), 0.0), axis=0, keepdims=True)


def one_hot(count, row):
    ids = iota((count, row.shape[1]), 0).astype(jnp.int16)
    return jnp.where(ids == row.astype(jnp.int16), jnp.ones((), BF16), jnp.zeros((), BF16))


def place_color(place):
    return (place >> 5) + ((place >> 3) & 3) + (place & 7)


def first_half():
    start = jnp.where(lax.axis_index("member") == 0, place_color(PATHS[0][0]), place_color(PATHS[1][0]))
    odd = (place_color(lax.axis_index("space")) + start) & 1
    return pl.multiple_of((1 - odd) * HALF_WIN, HALF_WIN), pl.multiple_of(odd * HALF_WIN, HALF_WIN)


def pack_kernel(
    var_count, x_hbm, eo_hbm, el_hbm, do_hbm, dl_hbm, w_hbm, block_hbm, out_ref, slot_ref, w_ref, states_ref,
    x_ref, eo_ref, el_ref, do_ref, dl_ref, block_ref, sems,
):
    members, _, pts = states_ref.shape
    n_dest = out_ref.shape[0]
    slots = n_dest * CAP
    pairs = [
        (eo_hbm, eo_ref),
        (do_hbm, do_ref),
        (el_hbm, el_ref),
        (dl_hbm, dl_ref),
        (x_hbm, x_ref),
        (w_hbm, w_ref),
        (block_hbm.at[lax.axis_index("member")], block_ref),
    ]
    copies = [pltpu.make_async_copy(src, dst, sems.at[i]) for i, (src, dst) in enumerate(pairs)]
    for copy in copies:
        copy.start()
    rows_in = members * var_count
    lanes = members * LANES
    row_id, col_id = iota((lanes, rows_in), 0), iota((lanes, rows_in), 1)
    var, m = row_id & (LANES - 1), row_id >> 7
    apart = ((var * members + m == col_id) & (var < var_count)).astype(F32).astype(BF16)
    copies[0].wait()
    copies[1].wait()
    copies[6].wait()
    owners = [eo_ref[...].astype(F32), do_ref[...].astype(F32)]
    block_of = column(block_ref[...])
    enc_slot, dec_slot = (
        (device_row(owner, block_of) * CAP + rank_row(owner)).astype(jnp.int32) for owner in owners
    )
    slot_ref[...] = dec_slot
    copies[2].wait()
    copies[3].wait()
    copies[4].wait()
    fields = jnp.dot(apart, x_ref[...].reshape(rows_in, pts), preferred_element_type=F32)
    for i in range(members):
        states_ref[i] = fields[i * LANES : i * LANES + var_count].astype(BF16)
    line_id = iota((lanes, pts), 0)
    fields += jnp.where(line_id == var_count, el_ref[...] + 1, 0).astype(F32)
    rows = nt_dot(one_hot(slots, enc_slot), fields.astype(BF16)).reshape(n_dest, CAP, lanes)
    rank = (dec_slot & (CAP - 1)) + META
    requests = jnp.where(iota((LANES, pts), 0) == rank, dl_ref[...] + 1, 0).astype(F32)
    asked = nt_dot(one_hot(n_dest, dec_slot >> CAP_BITS), requests.astype(BF16))
    top = iota((n_dest, CAP, LANES), 1) == 0
    asked = jnp.where(top, jnp.broadcast_to(asked[:, None, :], (n_dest, CAP, LANES)), 0.0)
    out_ref[:, :, 0:LANES] = rows[:, :, 0:LANES].astype(BF16)
    out_ref[:, :, LANES:] = (rows[:, :, LANES:] + asked).astype(BF16)
    copies[5].wait()
    w_ref[...] = w_ref[...] * jnp.asarray(0.5, BF16)


def encode_kernel(var_count, m, in_ref, w_ref, one_ref, two_ref, pooled_ref, ea_ref, eb_ref):
    n_dest = in_ref.shape[0]
    slots = n_dest * CAP
    width = w_ref.shape[1]
    nodes = NODE_DEV
    chunk = 256
    arrived = in_ref[...].reshape(slots, in_ref.shape[2])
    lane_id = iota((8, LANES), 1)
    pick = (lane_id == var_count).astype(F32).astype(BF16)
    node_row = nt_dot(pick, arrived[:, 0:LANES])[0:1, :]
    assign = one_hot(nodes, node_row.astype(jnp.int32) - 1)
    share = 1.0 / jnp.maximum(jnp.sum(assign.astype(F32), axis=1, keepdims=True), 1.0)
    x = arrived[:, m * LANES : m * LANES + var_count]

    def embed(c, e_ref):
        cols = pl.ds(pl.multiple_of(c * chunk, chunk), chunk)
        raw = jnp.dot(x, w_ref[:, cols], preferred_element_type=F32)
        e_ref[...] = (raw + raw * jnp.tanh(raw)).astype(BF16)

    def pool(c, e_ref):
        cols = pl.ds(pl.multiple_of(c * chunk, chunk), chunk)
        pooled_ref[:, cols] = jnp.dot(assign, e_ref[...], preferred_element_type=F32)

    chunks = width // chunk
    embed(0, ea_ref)
    for c in range(chunks):
        here, there = (ea_ref, eb_ref) if c % 2 == 0 else (eb_ref, ea_ref)
        if c + 1 < chunks:
            embed(c + 1, there)
        pool(c, here)
    step = 32
    odd = first_half()[0] == 0
    for r in range(0, HALF_WIN, step):
        lower, upper = slice(r, r + step), slice(HALF_WIN + r, HALF_WIN + r + step)
        halves = []
        for part in (lower, upper):
            summed, part_share = pooled_ref[part, :], share[part]
            centred = summed - jnp.mean(summed, axis=1, keepdims=True)
            variance = jnp.mean(centred * centred, axis=1, keepdims=True) * (part_share * part_share)
            halves.append((centred * (part_share * lax.rsqrt(variance + NORM_EPS))).astype(BF16))
        one_ref[lower, :] = jnp.where(odd, halves[0], halves[1])
        two_ref[lower, :] = jnp.where(odd, halves[1], halves[0])


def qkv_kernel(halves, *refs):
    hidden_refs, (w_ref, qk_ref, vt_ref, rows_ref) = refs[:halves], refs[halves:]
    width = rows_ref.shape[1]
    half = rows_ref.shape[0] // halves
    odd = first_half()[0] == 0
    for i in range(0, halves, 2):
        one, two = hidden_refs[i][...], hidden_refs[i + 1][...]
        rows_ref[i * half : (i + 1) * half, :] = jnp.where(odd, one, two)
        rows_ref[(i + 1) * half : (i + 2) * half, :] = jnp.where(odd, two, one)

    def project(cols):
        return jnp.dot(rows_ref[...], w_ref[:, cols], preferred_element_type=F32).astype(BF16)

    chunk = 512
    for c in range(0, 2 * width, chunk):
        qk_ref[:, c : c + chunk] = project(slice(c, c + chunk))
    for c in range(0, width, chunk):
        vt_ref[c : c + chunk, :] = project(slice(2 * width + c, 2 * width + c + chunk)).T


def attend_kernel(
    var_count, m, qk_ref, vt_ref, rows_ref, one_ref, two_ref, w_kv_ref, w_out_ref,
    w_dec_ref, *rest,
):
    if m == 0:
        out_ref, kh_ref, vth_ref, att_ref, proc_ref, left_ref, right_ref, sa_ref, sb_ref, e_ref, halo_ref = rest
    else:
        dec_ref, in_ref, out_ref, kh_ref, vth_ref, att_ref, proc_ref, left_ref, right_ref, sa_ref, sb_ref, e_ref, halo_ref, reply_ref = rest
    half, width = one_ref.shape
    core, me = lax.axis_index("member"), lax.axis_index("space")
    first_at = jnp.where(core == 0, PATHS[0][0], PATHS[1][0])
    last_at = jnp.where(core == 0, PATHS[0][-1], PATHS[1][-1])
    at_first, at_last = (me == first_at).astype(jnp.int32), (me == last_at).astype(jnp.int32)
    nodes = 2 * half
    head_dim = width // HEADS
    one, two = one_ref[...], two_ref[...]
    odd = first_half()[0] == 0
    halo_ref[0:half, :] = jnp.where(odd, one, two)
    halo_ref[half:, :] = jnp.where(odd, two, one)
    chunk = 256

    def project(c):
        k_src, v_src = slice(width + c, width + c + chunk), slice(2 * width + c, 2 * width + c + chunk)
        kh = jnp.dot(halo_ref[...], w_kv_ref[:, k_src], preferred_element_type=F32)
        kh_ref[:, c : c + chunk] = kh.astype(BF16)
        vh = jnp.dot(halo_ref[...], w_kv_ref[:, v_src], preferred_element_type=F32)
        vth_ref[c : c + chunk, :] = vh.astype(BF16).T

    key_id = iota((half, 2 * half), 0)
    query_id = iota((half, 2 * half), 1)
    query_id = jnp.where(query_id >= half, query_id - half, query_id)
    big = 4 * half
    zero, low = jnp.zeros((half, 2 * half), F32), jnp.full((half, 2 * half), -1e30, F32)
    left_ref[0] = jnp.where(key_id >= query_id + at_first * big, zero, low)
    left_ref[1] = jnp.where(key_id >= query_id, zero, low)
    right_ref[0] = jnp.where(key_id <= query_id, zero, low)
    right_ref[1] = jnp.where(key_id + at_last * big <= query_id, zero, low)
    even = iota((half, LANES), 1) < head_dim
    gain = head_dim ** (-0.5) * 1.4426950408889634
    base = m * nodes

    def scores(p, s_ref):
        cols = slice(p * LANES, (p + 1) * LANES)
        k_cols = slice(width + p * LANES, width + (p + 1) * LANES)
        k_own = qk_ref[base : base + nodes, k_cols]
        for side in range(2):
            row0 = side * half
            q = qk_ref[base + row0 : base + row0 + half, cols]
            none = jnp.zeros_like(q)
            q2 = jnp.concatenate([jnp.where(even, q, none), jnp.where(even, none, q)], axis=0)
            s_all = nt_dot(jnp.concatenate([k_own, kh_ref[row0 : row0 + half, cols]], axis=0), q2)
            s_own, s_halo = s_all[0:nodes], s_all[nodes:]
            if side == 0:
                s_ref[side, 0:half] = s_own[0:half]
                s_ref[side, half:nodes] = s_own[half:] + right_ref[0]
                s_ref[side, nodes:] = s_halo + left_ref[0]
            else:
                s_ref[side, 0:half] = s_own[0:half] + left_ref[1]
                s_ref[side, half:nodes] = s_own[half:]
                s_ref[side, nodes:] = s_halo + right_ref[1]

    def finish(p, s_ref):
        cols = slice(p * LANES, (p + 1) * LANES)
        blocks = (slice(0, half), slice(half, nodes), slice(nodes, nodes + half))
        for side in range(2):
            row0 = side * half
            s0, s1, s2 = (s_ref[side, b] for b in blocks)
            top = jnp.max(jnp.maximum(jnp.maximum(s0, s1), s2), axis=0, keepdims=True)
            total = None
            for b in blocks:
                e = jnp.exp2((s_ref[side, b] - top) * gain)
                e_ref[side, b] = e
                total = e if total is None else total + e
            inv = 1.0 / jnp.sum(total, axis=0, keepdims=True)
            p_own = (e_ref[side, 0:nodes] * inv).astype(BF16)
            p_halo = (e_ref[side, nodes:] * inv).astype(BF16)
            out = jnp.dot(vt_ref[cols, base : base + nodes], p_own, preferred_element_type=F32)
            out += jnp.dot(vth_ref[cols, row0 : row0 + half], p_halo, preferred_element_type=F32)
            pair = jnp.concatenate([out[0:head_dim, 0:half], out[head_dim:, half:]], axis=0)
            att_ref[row0 : row0 + half, cols] = pair.T.astype(BF16)

    if m == 1:
        n_dest = in_ref.shape[0]
        slots = n_dest * CAP
        cube = (n_dest, CAP, LANES)
        asked = in_ref[:, :, LANES:].astype(F32)
        asked = jnp.broadcast_to(asked[:, 0:1, :], cube)
        asked = jnp.where(iota(cube, 2) == iota(cube, 1) + META, asked, 0.0)
        asked = jnp.sum(asked, axis=2, keepdims=True).reshape(slots, 1)
        node_lane = (iota((slots, nodes), 1) + 1).astype(F32)
        reply_ref[...] = (node_lane == asked).astype(F32).astype(BF16)

    pairs = HEADS // 2
    per_chunk = chunk // LANES
    project(0)
    scores(0, sa_ref)
    for p in range(pairs):
        here, there = (sa_ref, sb_ref) if p % 2 == 0 else (sb_ref, sa_ref)
        if p % per_chunk == 0 and p + per_chunk < pairs:
            project((p // per_chunk + 1) * chunk)
        if p + 1 < pairs:
            scores(p + 1, there)
        finish(p, here)

    for c in range(0, width, chunk):
        cols = slice(c, c + chunk)
        mixed = jnp.dot(att_ref[...], w_out_ref[:, cols], preferred_element_type=F32)
        hidden = rows_ref[base : base + nodes, cols].astype(F32)
        proc_ref[:, cols] = (hidden + mixed).astype(BF16)
    decoded = nt_dot(proc_ref[...], w_dec_ref[...]).astype(BF16)
    if m == 0:
        out_ref[...] = jnp.zeros_like(out_ref)
        out_ref[:, 0:var_count] = decoded
    else:
        mine_ref = att_ref.at[:, 0:LANES]
        mine_ref[...] = jnp.zeros_like(mine_ref)
        mine_ref[:, 0:var_count] = decoded
        both = jnp.concatenate([dec_ref[...], mine_ref[...]], axis=1)
        reply = reply_ref[...]
        rows = jnp.dot(reply, both, preferred_element_type=F32).astype(BF16)
        out_ref[...] = rows.reshape(out_ref.shape)


def predict_kernel(var_count, slot_ref, back_ref, x_ref, out_ref):
    n_dest, _, lanes = back_ref.shape
    place = one_hot(n_dest * CAP, slot_ref[...])
    rows = back_ref[...].reshape(n_dest * CAP, lanes)
    got = lax.dot_general(rows, place, TN, preferred_element_type=F32)
    for m in range(x_ref.shape[0]):
        out_ref[m] = (x_ref[m].astype(F32) + got[m * LANES : m * LANES + var_count]).astype(BF16)


def score_kernel(mine_ref, other_ref, target_ref, out_hbm, out_ref, sems):
    refs = [(r, m) for r in (mine_ref, other_ref) for m in range(mine_ref.shape[0])]
    count = len(refs)
    fair_eps = (1.0 - FAIR_ALPHA) / count
    weight = (1.0 - fair_eps) / (2.0 * count * (count - 1)) * 2.0
    edges = [0, 32, 64, out_ref.shape[0]]
    copies = []
    for i, (lo, hi) in enumerate(zip(edges, edges[1:])):
        fields = [r[m, lo:hi].astype(F32) for r, m in refs]
        target = target_ref[lo:hi]
        skill = sum(jnp.abs(f - target) for f in fields) / count
        spread = sum(
            jnp.abs(fields[i] - fields[j]) for i in range(count) for j in range(i + 1, count)
        )
        out_ref[lo:hi] = skill - weight * spread
        rows = pl.ds(lo, hi - lo)
        copies.append(pltpu.make_async_copy(out_ref.at[rows], out_hbm.at[rows], sems.at[i]))
        copies[-1].start()
    for copy in copies:
        copy.wait()


def params(mib=32):
    return pltpu.CompilerParams(vmem_limit_bytes=mib << 20)


def cost(micros):
    return pl.CostEstimate(flops=int(micros * 7e8), bytes_accessed=1 << 20, transcendentals=0)


def on_device(
    initial_states,
    target,
    enc_owner,
    enc_local,
    dec_owner,
    dec_local,
    w_embed,
    w_qkv,
    w_out,
    w_decode,
):
    n_space = lax.axis_size("space")
    members, pts, var_count = initial_states.shape
    width = w_embed.shape[1]
    nodes, half = NODE_DEV, HALF_WIN
    slots = n_space * CAP
    in_hbm = functools.partial(pltpu.with_memory_space_constraint, memory_space=pltpu.HBM)
    rows = [in_hbm(a.reshape(1, pts)) for a in (enc_owner, enc_local, dec_owner, dec_local)]
    wire = jax.ShapeDtypeStruct((n_space, CAP, members * LANES), BF16)

    block_of = np.zeros((len(PATHS), 1, n_space), np.float32)
    for core, path in enumerate(PATHS):
        block_of[core, 0, list(path)] = np.arange(n_space)
    row_shape = pltpu.VMEM((1, pts), jnp.int32)
    outgoing, dec_slot, w_enc, states = pl.pallas_call(
        functools.partial(pack_kernel, var_count),
        in_specs=[HBM_SPEC] * 7,
        out_shape=(
            wire,
            jax.ShapeDtypeStruct((1, pts), jnp.int32),
            jax.ShapeDtypeStruct(w_embed.shape, BF16),
            jax.ShapeDtypeStruct((members, var_count, pts), BF16),
        ),
        scratch_shapes=[pltpu.VMEM((var_count, members, pts), BF16)]
        + [row_shape] * 4
        + [pltpu.VMEM((1, n_space), F32), pltpu.SemaphoreType.DMA((7,))],
        compiler_params=params(),
        cost_estimate=cost(2),
        name="pack",
    )(in_hbm(jnp.transpose(initial_states, (2, 0, 1))), *rows, in_hbm(w_embed), in_hbm(jnp.asarray(block_of)))
    arrived = lax.all_to_all(outgoing, "space", 0, 0, tiled=True)

    half_shape = jax.ShapeDtypeStruct((half, width), BF16)
    swaps = [[], []]
    for c, path in enumerate(PATHS):
        for i, a in enumerate(path):
            b = path[(i + 1) % n_space]
            swaps[i % 2] += [(c * n_space + a, c * n_space + b), (c * n_space + b, c * n_space + a)]
    both_axes = ("member", "space")
    hidden, halos = [], []
    for m in range(members):
        ends = pl.pallas_call(
            functools.partial(encode_kernel, var_count, m),
            out_shape=(half_shape, half_shape),
            scratch_shapes=[pltpu.VMEM((nodes, width), F32)] + [pltpu.VMEM((slots, 256), BF16)] * 2,
            compiler_params=params(),
            cost_estimate=cost(3),
            name=f"encode{m}",
        )(arrived, w_enc)
        hidden += ends
        halos.append([lax.ppermute(end, both_axes, swap) for end, swap in zip(ends, swaps)])

    qk, vt, node_rows = pl.pallas_call(
        functools.partial(qkv_kernel, len(hidden)),
        out_shape=(
            jax.ShapeDtypeStruct((members * nodes, 2 * width), BF16),
            jax.ShapeDtypeStruct((width, members * nodes), BF16),
            jax.ShapeDtypeStruct((members * nodes, width), BF16),
        ),
        cost_estimate=cost(5),
        compiler_params=params(),
        name="qkv",
    )(*hidden, w_qkv)

    decoded = None
    for m in range(members):
        extra = () if m == 0 else (decoded, arrived)
        decoded = pl.pallas_call(
            functools.partial(attend_kernel, var_count, m),
            out_shape=jax.ShapeDtypeStruct((nodes, LANES), BF16) if m == 0 else wire,
            scratch_shapes=[
                pltpu.VMEM((nodes, width), BF16),
                pltpu.VMEM((width, nodes), BF16),
                pltpu.VMEM((nodes, width), BF16),
                pltpu.VMEM((nodes, width), BF16),
                pltpu.VMEM((2, half, nodes), F32),
                pltpu.VMEM((2, half, nodes), F32),
                pltpu.VMEM((2, nodes + half, nodes), F32),
                pltpu.VMEM((2, nodes + half, nodes), F32),
                pltpu.VMEM((2, nodes + half, nodes), F32),
                pltpu.VMEM((nodes, width), BF16),
            ]
            + [pltpu.VMEM((slots, nodes), BF16)] * m,
            compiler_params=params(),
            cost_estimate=cost(8),
            name=f"attend{m}",
        )(qk, vt, node_rows, *halos[m], w_qkv, w_out, w_decode.T, *extra)
    replies = decoded

    returned = lax.all_to_all(replies, "space", 0, 0, tiled=True)
    predicted = pl.pallas_call(
        functools.partial(predict_kernel, var_count),
        out_shape=jax.ShapeDtypeStruct((members, var_count, pts), BF16),
        compiler_params=params(),
        name="predict",
    )(dec_slot, returned, states)
    other = lax.ppermute(predicted, "member", [(0, 1), (1, 0)])
    error = pl.pallas_call(
        score_kernel,
        in_specs=[VMEM_SPEC] * 3,
        out_specs=HBM_SPEC,
        out_shape=jax.ShapeDtypeStruct((var_count, pts), F32),
        scratch_shapes=[pltpu.VMEM((var_count, pts), F32), pltpu.SemaphoreType.DMA((3,))],
        compiler_params=params(),
        name="score",
    )(predicted, other, target.T)
    return jnp.transpose(predicted, (0, 2, 1)), error.T


def solution(mesh):
    in_specs = (
        P("member", "space", None),
        P("space", None),
        P("space", None),
        P("space", None),
        P("space", None),
        P("space", None),
        P(),
        P(),
        P(),
        P(),
    )
    out_specs = (P("member", "space", None), P("space", None))
    return jax.shard_map(
        on_device, mesh=mesh, in_specs=in_specs, out_specs=out_specs, check_vma=False
    )
```

```python
import functools

import jax
import jax.numpy as jnp
from jax import lax
from jax.experimental import pallas as pl
from jax.experimental.pallas import tpu as pltpu
from jax.sharding import PartitionSpec as P

HEADS = 16
HALF_WIN = 128
NODE_DEV = 256
CAP = 8
CAP_BITS = 3
META = 104
LANES = 128
GRID = (4, 4, 8)
Y_BITS, Z_BITS = 2, 3

FAIR_ALPHA = 0.95
NORM_EPS = 1e-05

F32 = jnp.float32
BF16 = jnp.bfloat16
NT = (((1,), (1,)), ((), ()))
TN = (((0,), (0,)), ((), ()))
VMEM_SPEC = pl.BlockSpec(memory_space=pltpu.VMEM)
HBM_SPEC = pl.BlockSpec(memory_space=pltpu.HBM)


def nt_dot(a, b):
    return lax.dot_general(a, b, NT, preferred_element_type=F32)


def iota(shape, dim):
    return lax.broadcasted_iota(jnp.int32, shape, dim)


def column(row):
    return jnp.broadcast_to(row, (8, row.shape[1])).T[:, 0:1]


def rank_row(owner):
    pts = owner.shape[1]
    owner_col = column(owner)
    block = LANES
    ahead = iota((block, block), 0) < iota((block, block), 1)
    ranks = []
    for c in range(0, pts, block):
        wide = jnp.broadcast_to(owner[:, c : c + block], (block, block))
        count = jnp.where(ahead & (owner_col[c : c + block] == wide), 1.0, 0.0)
        for r in range(0, c, block):
            count += jnp.where(owner_col[r : r + block] == wide, 1.0, 0.0)
        ranks.append(jnp.sum(count, axis=0, keepdims=True))
    return jnp.concatenate(ranks, axis=1)


def path_place(block):
    _, ny, nz = GRID
    line, z = block >> Z_BITS, block & (nz - 1)
    x, y = line >> Y_BITS, line & (ny - 1)
    z = z + (line & 1) * (nz - 1 - 2 * z)
    y = y + (x & 1) * (ny - 1 - 2 * y)
    return (((x << Y_BITS) + y) << Z_BITS) + z


def one_hot(count, row):
    ids = iota((count, row.shape[1]), 0).astype(jnp.int16)
    return jnp.where(ids == row.astype(jnp.int16), jnp.ones((), BF16), jnp.zeros((), BF16))


def place_color(place):
    return (place >> 5) + ((place >> 3) & 3) + (place & 7)


def first_half():
    odd = place_color(lax.axis_index("space")) & 1
    return pl.multiple_of((1 - odd) * HALF_WIN, HALF_WIN), pl.multiple_of(odd * HALF_WIN, HALF_WIN)


def pack_kernel(
    var_count, x_hbm, eo_hbm, el_hbm, do_hbm, dl_hbm, w_hbm, out_ref, slot_ref, w_ref, states_ref,
    x_ref, eo_ref, el_ref, do_ref, dl_ref, sems,
):
    members, _, pts = states_ref.shape
    n_dest = out_ref.shape[0]
    slots = n_dest * CAP
    pairs = [
        (eo_hbm, eo_ref),
        (do_hbm, do_ref),
        (el_hbm, el_ref),
        (dl_hbm, dl_ref),
        (x_hbm, x_ref),
        (w_hbm, w_ref),
    ]
    copies = [pltpu.make_async_copy(src, dst, sems.at[i]) for i, (src, dst) in enumerate(pairs)]
    for copy in copies:
        copy.start()
    rows_in = members * var_count
    lanes = members * LANES
    row_id, col_id = iota((lanes, rows_in), 0), iota((lanes, rows_in), 1)
    var, m = row_id & (LANES - 1), row_id >> 7
    apart = ((var * members + m == col_id) & (var < var_count)).astype(F32).astype(BF16)
    copies[0].wait()
    copies[1].wait()
    enc_slot, dec_slot = (
        path_place(ref[...]) * CAP + rank_row(ref[...].astype(F32)).astype(jnp.int32)
        for ref in (eo_ref, do_ref)
    )
    slot_ref[...] = dec_slot
    copies[2].wait()
    copies[3].wait()
    copies[4].wait()
    fields = jnp.dot(apart, x_ref[...].reshape(rows_in, pts), preferred_element_type=F32)
    for i in range(members):
        states_ref[i] = fields[i * LANES : i * LANES + var_count].astype(BF16)
    line_id = iota((lanes, pts), 0)
    fields += jnp.where(line_id == var_count, el_ref[...] + 1, 0).astype(F32)
    rows = nt_dot(one_hot(slots, enc_slot), fields.astype(BF16)).reshape(n_dest, CAP, lanes)
    rank = (dec_slot & (CAP - 1)) + META
    requests = jnp.where(iota((LANES, pts), 0) == rank, dl_ref[...] + 1, 0).astype(F32)
    asked = nt_dot(one_hot(n_dest, dec_slot >> CAP_BITS), requests.astype(BF16))
    top = iota((n_dest, CAP, LANES), 1) == 0
    asked = jnp.where(top, jnp.broadcast_to(asked[:, None, :], (n_dest, CAP, LANES)), 0.0)
    out_ref[:, :, 0:LANES] = rows[:, :, 0:LANES].astype(BF16)
    out_ref[:, :, LANES:] = (rows[:, :, LANES:] + asked).astype(BF16)
    copies[5].wait()
    w_ref[...] = w_ref[...] * jnp.asarray(0.5, BF16)


def encode_kernel(var_count, m, in_ref, w_ref, one_ref, two_ref, pooled_ref, ea_ref, eb_ref):
    n_dest = in_ref.shape[0]
    slots = n_dest * CAP
    width = w_ref.shape[1]
    nodes = NODE_DEV
    chunk = 256
    arrived = in_ref[...].reshape(slots, in_ref.shape[2])
    lane_id = iota((8, LANES), 1)
    pick = (lane_id == var_count).astype(F32).astype(BF16)
    node_row = nt_dot(pick, arrived[:, 0:LANES])[0:1, :]
    assign = one_hot(nodes, node_row.astype(jnp.int32) - 1)
    share = 1.0 / jnp.maximum(jnp.sum(assign.astype(F32), axis=1, keepdims=True), 1.0)
    x = arrived[:, m * LANES : m * LANES + var_count]

    def embed(c, e_ref):
        cols = pl.ds(pl.multiple_of(c * chunk, chunk), chunk)
        raw = jnp.dot(x, w_ref[:, cols], preferred_element_type=F32)
        e_ref[...] = (raw + raw * jnp.tanh(raw)).astype(BF16)

    def pool(c, e_ref):
        cols = pl.ds(pl.multiple_of(c * chunk, chunk), chunk)
        pooled_ref[:, cols] = jnp.dot(assign, e_ref[...], preferred_element_type=F32)

    chunks = width // chunk
    embed(0, ea_ref)
    for c in range(chunks):
        here, there = (ea_ref, eb_ref) if c % 2 == 0 else (eb_ref, ea_ref)
        if c + 1 < chunks:
            embed(c + 1, there)
        pool(c, here)
    step = 32
    odd = first_half()[0] == 0
    for r in range(0, HALF_WIN, step):
        lower, upper = slice(r, r + step), slice(HALF_WIN + r, HALF_WIN + r + step)
        halves = []
        for part in (lower, upper):
            summed, part_share = pooled_ref[part, :], share[part]
            centred = summed - jnp.mean(summed, axis=1, keepdims=True)
            variance = jnp.mean(centred * centred, axis=1, keepdims=True) * (part_share * part_share)
            halves.append((centred * (part_share * lax.rsqrt(variance + NORM_EPS))).astype(BF16))
        one_ref[lower, :] = jnp.where(odd, halves[0], halves[1])
        two_ref[lower, :] = jnp.where(odd, halves[1], halves[0])


def qkv_kernel(halves, *refs):
    hidden_refs, (w_ref, qk_ref, vt_ref, rows_ref) = refs[:halves], refs[halves:]
    width = rows_ref.shape[1]
    half = rows_ref.shape[0] // halves
    odd = first_half()[0] == 0
    for i in range(0, halves, 2):
        one, two = hidden_refs[i][...], hidden_refs[i + 1][...]
        rows_ref[i * half : (i + 1) * half, :] = jnp.where(odd, one, two)
        rows_ref[(i + 1) * half : (i + 2) * half, :] = jnp.where(odd, two, one)

    def project(cols):
        return jnp.dot(rows_ref[...], w_ref[:, cols], preferred_element_type=F32).astype(BF16)

    chunk = 512
    for c in range(0, 2 * width, chunk):
        qk_ref[:, c : c + chunk] = project(slice(c, c + chunk))
    for c in range(0, width, chunk):
        vt_ref[c : c + chunk, :] = project(slice(2 * width + c, 2 * width + c + chunk)).T


def attend_kernel(
    var_count, m, qk_ref, vt_ref, rows_ref, one_ref, two_ref, w_kv_ref, w_out_ref,
    w_dec_ref, *rest,
):
    if m == 0:
        out_ref, kh_ref, vth_ref, att_ref, proc_ref, left_ref, right_ref, sa_ref, sb_ref, e_ref, halo_ref = rest
    else:
        dec_ref, in_ref, out_ref, kh_ref, vth_ref, att_ref, proc_ref, left_ref, right_ref, sa_ref, sb_ref, e_ref, halo_ref, reply_ref = rest
    half, width = one_ref.shape
    me = lax.axis_index("space")
    at_first, at_last = (me == path_place(0)).astype(jnp.int32), (me == path_place((1 << 7) - 1)).astype(jnp.int32)
    nodes = 2 * half
    head_dim = width // HEADS
    one, two = one_ref[...], two_ref[...]
    odd = first_half()[0] == 0
    halo_ref[0:half, :] = jnp.where(odd, one, two)
    halo_ref[half:, :] = jnp.where(odd, two, one)
    chunk = 256

    def project(c):
        k_src, v_src = slice(width + c, width + c + chunk), slice(2 * width + c, 2 * width + c + chunk)
        kh = jnp.dot(halo_ref[...], w_kv_ref[:, k_src], preferred_element_type=F32)
        kh_ref[:, c : c + chunk] = kh.astype(BF16)
        vh = jnp.dot(halo_ref[...], w_kv_ref[:, v_src], preferred_element_type=F32)
        vth_ref[c : c + chunk, :] = vh.astype(BF16).T

    key_id = iota((half, 2 * half), 0)
    query_id = iota((half, 2 * half), 1)
    query_id = jnp.where(query_id >= half, query_id - half, query_id)
    big = 4 * half
    zero, low = jnp.zeros((half, 2 * half), F32), jnp.full((half, 2 * half), -1e30, F32)
    left_ref[0] = jnp.where(key_id >= query_id + at_first * big, zero, low)
    left_ref[1] = jnp.where(key_id >= query_id, zero, low)
    right_ref[0] = jnp.where(key_id <= query_id, zero, low)
    right_ref[1] = jnp.where(key_id + at_last * big <= query_id, zero, low)
    even = iota((half, LANES), 1) < head_dim
    gain = head_dim ** (-0.5) * 1.4426950408889634
    base = m * nodes

    def scores(p, s_ref):
        cols = slice(p * LANES, (p + 1) * LANES)
        k_cols = slice(width + p * LANES, width + (p + 1) * LANES)
        k_own = qk_ref[base : base + nodes, k_cols]
        for side in range(2):
            row0 = side * half
            q = qk_ref[base + row0 : base + row0 + half, cols]
            none = jnp.zeros_like(q)
            q2 = jnp.concatenate([jnp.where(even, q, none), jnp.where(even, none, q)], axis=0)
            s_all = nt_dot(jnp.concatenate([k_own, kh_ref[row0 : row0 + half, cols]], axis=0), q2)
            s_own, s_halo = s_all[0:nodes], s_all[nodes:]
            if side == 0:
                s_ref[side, 0:half] = s_own[0:half]
                s_ref[side, half:nodes] = s_own[half:] + right_ref[0]
                s_ref[side, nodes:] = s_halo + left_ref[0]
            else:
                s_ref[side, 0:half] = s_own[0:half] + left_ref[1]
                s_ref[side, half:nodes] = s_own[half:]
                s_ref[side, nodes:] = s_halo + right_ref[1]

    def finish(p, s_ref):
        cols = slice(p * LANES, (p + 1) * LANES)
        blocks = (slice(0, half), slice(half, nodes), slice(nodes, nodes + half))
        for side in range(2):
            row0 = side * half
            s0, s1, s2 = (s_ref[side, b] for b in blocks)
            top = jnp.max(jnp.maximum(jnp.maximum(s0, s1), s2), axis=0, keepdims=True)
            total = None
            for b in blocks:
                e = jnp.exp2((s_ref[side, b] - top) * gain)
                e_ref[side, b] = e
                total = e if total is None else total + e
            inv = 1.0 / jnp.sum(total, axis=0, keepdims=True)
            p_own = (e_ref[side, 0:nodes] * inv).astype(BF16)
            p_halo = (e_ref[side, nodes:] * inv).astype(BF16)
            out = jnp.dot(vt_ref[cols, base : base + nodes], p_own, preferred_element_type=F32)
            out += jnp.dot(vth_ref[cols, row0 : row0 + half], p_halo, preferred_element_type=F32)
            pair = jnp.concatenate([out[0:head_dim, 0:half], out[head_dim:, half:]], axis=0)
            att_ref[row0 : row0 + half, cols] = pair.T.astype(BF16)

    if m == 1:
        n_dest = in_ref.shape[0]
        slots = n_dest * CAP
        cube = (n_dest, CAP, LANES)
        asked = in_ref[:, :, LANES:].astype(F32)
        asked = jnp.broadcast_to(asked[:, 0:1, :], cube)
        asked = jnp.where(iota(cube, 2) == iota(cube, 1) + META, asked, 0.0)
        asked = jnp.sum(asked, axis=2, keepdims=True).reshape(slots, 1)
        node_lane = (iota((slots, nodes), 1) + 1).astype(F32)
        reply_ref[...] = (node_lane == asked).astype(F32).astype(BF16)

    pairs = HEADS // 2
    per_chunk = chunk // LANES
    project(0)
    scores(0, sa_ref)
    for p in range(pairs):
        here, there = (sa_ref, sb_ref) if p % 2 == 0 else (sb_ref, sa_ref)
        if p % per_chunk == 0 and p + per_chunk < pairs:
            project((p // per_chunk + 1) * chunk)
        if p + 1 < pairs:
            scores(p + 1, there)
        finish(p, here)

    for c in range(0, width, chunk):
        cols = slice(c, c + chunk)
        mixed = jnp.dot(att_ref[...], w_out_ref[:, cols], preferred_element_type=F32)
        hidden = rows_ref[base : base + nodes, cols].astype(F32)
        proc_ref[:, cols] = (hidden + mixed).astype(BF16)
    decoded = nt_dot(proc_ref[...], w_dec_ref[...]).astype(BF16)
    if m == 0:
        out_ref[...] = jnp.zeros_like(out_ref)
        out_ref[:, 0:var_count] = decoded
    else:
        mine_ref = att_ref.at[:, 0:LANES]
        mine_ref[...] = jnp.zeros_like(mine_ref)
        mine_ref[:, 0:var_count] = decoded
        both = jnp.concatenate([dec_ref[...], mine_ref[...]], axis=1)
        reply = reply_ref[...]
        rows = jnp.dot(reply, both, preferred_element_type=F32).astype(BF16)
        out_ref[...] = rows.reshape(out_ref.shape)


def predict_kernel(var_count, slot_ref, back_ref, x_ref, out_ref):
    n_dest, _, lanes = back_ref.shape
    place = one_hot(n_dest * CAP, slot_ref[...])
    rows = back_ref[...].reshape(n_dest * CAP, lanes)
    got = lax.dot_general(rows, place, TN, preferred_element_type=F32)
    for m in range(x_ref.shape[0]):
        out_ref[m] = (x_ref[m].astype(F32) + got[m * LANES : m * LANES + var_count]).astype(BF16)


def score_kernel(mine_ref, other_ref, target_ref, out_hbm, out_ref, sems):
    refs = [(r, m) for r in (mine_ref, other_ref) for m in range(mine_ref.shape[0])]
    count = len(refs)
    fair_eps = (1.0 - FAIR_ALPHA) / count
    weight = (1.0 - fair_eps) / (2.0 * count * (count - 1)) * 2.0
    edges = [0, 32, 64, out_ref.shape[0]]
    copies = []
    for i, (lo, hi) in enumerate(zip(edges, edges[1:])):
        fields = [r[m, lo:hi].astype(F32) for r, m in refs]
        target = target_ref[lo:hi]
        skill = sum(jnp.abs(f - target) for f in fields) / count
        spread = sum(
            jnp.abs(fields[i] - fields[j]) for i in range(count) for j in range(i + 1, count)
        )
        out_ref[lo:hi] = skill - weight * spread
        rows = pl.ds(lo, hi - lo)
        copies.append(pltpu.make_async_copy(out_ref.at[rows], out_hbm.at[rows], sems.at[i]))
        copies[-1].start()
    for copy in copies:
        copy.wait()


def params(mib=32):
    return pltpu.CompilerParams(vmem_limit_bytes=mib << 20)


def cost(micros):
    return pl.CostEstimate(flops=int(micros * 7e8), bytes_accessed=1 << 20, transcendentals=0)


def on_device(
    initial_states,
    target,
    enc_owner,
    enc_local,
    dec_owner,
    dec_local,
    w_embed,
    w_qkv,
    w_out,
    w_decode,
):
    n_space = lax.axis_size("space")
    members, pts, var_count = initial_states.shape
    width = w_embed.shape[1]
    nodes, half = NODE_DEV, HALF_WIN
    slots = n_space * CAP
    in_hbm = functools.partial(pltpu.with_memory_space_constraint, memory_space=pltpu.HBM)
    rows = [in_hbm(a.reshape(1, pts)) for a in (enc_owner, enc_local, dec_owner, dec_local)]
    wire = jax.ShapeDtypeStruct((n_space, CAP, members * LANES), BF16)

    path = [path_place(b) for b in range(n_space)]
    row_shape = pltpu.VMEM((1, pts), jnp.int32)
    outgoing, dec_slot, w_enc, states = pl.pallas_call(
        functools.partial(pack_kernel, var_count),
        in_specs=[HBM_SPEC] * 6,
        out_shape=(
            wire,
            jax.ShapeDtypeStruct((1, pts), jnp.int32),
            jax.ShapeDtypeStruct(w_embed.shape, BF16),
            jax.ShapeDtypeStruct((members, var_count, pts), BF16),
        ),
        scratch_shapes=[pltpu.VMEM((var_count, members, pts), BF16)]
        + [row_shape] * 4
        + [pltpu.SemaphoreType.DMA((6,))],
        compiler_params=params(),
        cost_estimate=cost(2),
        name="pack",
    )(in_hbm(jnp.transpose(initial_states, (2, 0, 1))), *rows, in_hbm(w_embed))
    arrived = lax.all_to_all(outgoing, "space", 0, 0, tiled=True)

    half_shape = jax.ShapeDtypeStruct((half, width), BF16)
    swaps = [[], []]
    for i, a in enumerate(path):
        b = path[(i + 1) % n_space]
        swaps[i % 2] += [(a, b), (b, a)]
    hidden, halos = [], []
    for m in range(members):
        ends = pl.pallas_call(
            functools.partial(encode_kernel, var_count, m),
            out_shape=(half_shape, half_shape),
            scratch_shapes=[pltpu.VMEM((nodes, width), F32)] + [pltpu.VMEM((slots, 256), BF16)] * 2,
            compiler_params=params(),
            cost_estimate=cost(3),
            name=f"encode{m}",
        )(arrived, w_enc)
        hidden += ends
        halos.append([lax.ppermute(end, "space", swap) for end, swap in zip(ends, swaps)])

    qk, vt, node_rows = pl.pallas_call(
        functools.partial(qkv_kernel, len(hidden)),
        out_shape=(
            jax.ShapeDtypeStruct((members * nodes, 2 * width), BF16),
            jax.ShapeDtypeStruct((width, members * nodes), BF16),
            jax.ShapeDtypeStruct((members * nodes, width), BF16),
        ),
        cost_estimate=cost(5),
        compiler_params=params(),
        name="qkv",
    )(*hidden, w_qkv)

    decoded = None
    for m in range(members):
        extra = () if m == 0 else (decoded, arrived)
        decoded = pl.pallas_call(
            functools.partial(attend_kernel, var_count, m),
            out_shape=jax.ShapeDtypeStruct((nodes, LANES), BF16) if m == 0 else wire,
            scratch_shapes=[
                pltpu.VMEM((nodes, width), BF16),
                pltpu.VMEM((width, nodes), BF16),
                pltpu.VMEM((nodes, width), BF16),
                pltpu.VMEM((nodes, width), BF16),
                pltpu.VMEM((2, half, nodes), F32),
                pltpu.VMEM((2, half, nodes), F32),
                pltpu.VMEM((2, nodes + half, nodes), F32),
                pltpu.VMEM((2, nodes + half, nodes), F32),
                pltpu.VMEM((2, nodes + half, nodes), F32),
                pltpu.VMEM((nodes, width), BF16),
            ]
            + [pltpu.VMEM((slots, nodes), BF16)] * m,
            compiler_params=params(),
            cost_estimate=cost(8),
            name=f"attend{m}",
        )(qk, vt, node_rows, *halos[m], w_qkv, w_out, w_decode.T, *extra)
    replies = decoded

    returned = lax.all_to_all(replies, "space", 0, 0, tiled=True)
    predicted = pl.pallas_call(
        functools.partial(predict_kernel, var_count),
        out_shape=jax.ShapeDtypeStruct((members, var_count, pts), BF16),
        compiler_params=params(),
        name="predict",
    )(dec_slot, returned, states)
    other = lax.ppermute(predicted, "member", [(0, 1), (1, 0)])
    error = pl.pallas_call(
        score_kernel,
        in_specs=[VMEM_SPEC] * 3,
        out_specs=HBM_SPEC,
        out_shape=jax.ShapeDtypeStruct((var_count, pts), F32),
        scratch_shapes=[pltpu.VMEM((var_count, pts), F32), pltpu.SemaphoreType.DMA((3,))],
        compiler_params=params(),
        name="score",
    )(predicted, other, target.T)
    return jnp.transpose(predicted, (0, 2, 1)), error.T


def solution(mesh):
    in_specs = (
        P("member", "space", None),
        P("space", None),
        P("space", None),
        P("space", None),
        P("space", None),
        P("space", None),
        P(),
        P(),
        P(),
        P(),
    )
    out_specs = (P("member", "space", None), P("space", None))
    return jax.shard_map(
        on_device, mesh=mesh, in_specs=in_specs, out_specs=out_specs, check_vma=False
    )
```

```python
import functools

import jax
import jax.numpy as jnp
from jax import lax
from jax.experimental import pallas as pl
from jax.experimental.pallas import tpu as pltpu
from jax.sharding import PartitionSpec as P

HEADS = 16
HALF_WIN = 128
NODE_DEV = 256
CAP = 8
CAP_BITS = 3
META = 104
LANES = 128
GRID = (4, 4, 8)
Y_BITS, Z_BITS = 2, 3

FAIR_ALPHA = 0.95
NORM_EPS = 1e-05

F32 = jnp.float32
BF16 = jnp.bfloat16
NT = (((1,), (1,)), ((), ()))
TN = (((0,), (0,)), ((), ()))
VMEM_SPEC = pl.BlockSpec(memory_space=pltpu.VMEM)
HBM_SPEC = pl.BlockSpec(memory_space=pltpu.HBM)


def nt_dot(a, b):
    return lax.dot_general(a, b, NT, preferred_element_type=F32)


def iota(shape, dim):
    return lax.broadcasted_iota(jnp.int32, shape, dim)


def column(row):
    return jnp.broadcast_to(row, (8, row.shape[1])).T[:, 0:1]


def rank_row(owner):
    pts = owner.shape[1]
    owner_col = column(owner)
    block = LANES
    ahead = iota((block, block), 0) < iota((block, block), 1)
    ranks = []
    for c in range(0, pts, block):
        wide = jnp.broadcast_to(owner[:, c : c + block], (block, block))
        count = jnp.where(ahead & (owner_col[c : c + block] == wide), 1.0, 0.0)
        for r in range(0, c, block):
            count += jnp.where(owner_col[r : r + block] == wide, 1.0, 0.0)
        ranks.append(jnp.sum(count, axis=0, keepdims=True))
    return jnp.concatenate(ranks, axis=1)


def path_place(block):
    _, ny, nz = GRID
    line, z = block >> Z_BITS, block & (nz - 1)
    x, y = line >> Y_BITS, line & (ny - 1)
    z = z + (line & 1) * (nz - 1 - 2 * z)
    y = y + (x & 1) * (ny - 1 - 2 * y)
    return (((x << Y_BITS) + y) << Z_BITS) + z


def one_hot(count, row):
    ids = iota((count, row.shape[1]), 0).astype(jnp.int16)
    return jnp.where(ids == row.astype(jnp.int16), jnp.ones((), BF16), jnp.zeros((), BF16))


def place_color(place):
    return (place >> 5) + ((place >> 3) & 3) + (place & 7)


def first_half():
    odd = place_color(lax.axis_index("space")) & 1
    return pl.multiple_of((1 - odd) * HALF_WIN, HALF_WIN), pl.multiple_of(odd * HALF_WIN, HALF_WIN)


def pack_kernel(
    var_count, x_hbm, eo_hbm, el_hbm, do_hbm, dl_hbm, w_hbm, out_ref, slot_ref, w_ref, states_ref, left_ref, right_ref,
    x_ref, eo_ref, el_ref, do_ref, dl_ref, sems,
):
    members, _, pts = states_ref.shape
    n_dest = out_ref.shape[0]
    slots = n_dest * CAP
    pairs = [
        (eo_hbm, eo_ref),
        (do_hbm, do_ref),
        (el_hbm, el_ref),
        (dl_hbm, dl_ref),
        (x_hbm, x_ref),
        (w_hbm, w_ref),
    ]
    copies = [pltpu.make_async_copy(src, dst, sems.at[i]) for i, (src, dst) in enumerate(pairs)]
    for copy in copies:
        copy.start()
    me = lax.axis_index("space")
    at_first = (me == path_place(0)).astype(jnp.int32)
    at_last = (me == path_place((1 << 7) - 1)).astype(jnp.int32)
    _, half, across = left_ref.shape
    key_id = iota((half, across), 0)
    query_id = iota((half, across), 1) & (half - 1)
    zero, low = jnp.zeros((half, across), F32), jnp.full((half, across), -1e30, F32)
    left_ref[0] = jnp.where(key_id >= query_id + at_first * across, zero, low)
    left_ref[1] = jnp.where(key_id >= query_id, zero, low)
    right_ref[0] = jnp.where(key_id <= query_id, zero, low)
    right_ref[1] = jnp.where(key_id + at_last * across <= query_id, zero, low)
    rows_in = members * var_count
    lanes = members * LANES
    row_id, col_id = iota((lanes, rows_in), 0), iota((lanes, rows_in), 1)
    var, m = row_id & (LANES - 1), row_id >> 7
    apart = ((var * members + m == col_id) & (var < var_count)).astype(F32).astype(BF16)
    copies[0].wait()
    copies[1].wait()
    enc_slot, dec_slot = (
        path_place(ref[...]) * CAP + rank_row(ref[...].astype(F32)).astype(jnp.int32)
        for ref in (eo_ref, do_ref)
    )
    slot_ref[...] = dec_slot
    copies[2].wait()
    copies[3].wait()
    copies[4].wait()
    fields = jnp.dot(apart, x_ref[...].reshape(rows_in, pts), preferred_element_type=F32)
    for i in range(members):
        states_ref[i] = fields[i * LANES : i * LANES + var_count].astype(BF16)
    line_id = iota((lanes, pts), 0)
    fields += jnp.where(line_id == var_count, el_ref[...] + 1, 0).astype(F32)
    rows = nt_dot(one_hot(slots, enc_slot), fields.astype(BF16)).reshape(n_dest, CAP, lanes)
    rank = (dec_slot & (CAP - 1)) + META
    requests = jnp.where(iota((LANES, pts), 0) == rank, dl_ref[...] + 1, 0).astype(F32)
    asked = nt_dot(one_hot(n_dest, dec_slot >> CAP_BITS), requests.astype(BF16))
    top = iota((n_dest, CAP, LANES), 1) == 0
    asked = jnp.where(top, jnp.broadcast_to(asked[:, None, :], (n_dest, CAP, LANES)), 0.0)
    out_ref[:, :, 0:LANES] = rows[:, :, 0:LANES].astype(BF16)
    out_ref[:, :, LANES:] = (rows[:, :, LANES:] + asked).astype(BF16)
    copies[5].wait()
    w_ref[...] = w_ref[...] * jnp.asarray(0.5, BF16)


def encode_kernel(var_count, m, in_ref, w_ref, one_ref, two_ref, pooled_ref, ea_ref, eb_ref):
    n_dest = in_ref.shape[0]
    slots = n_dest * CAP
    width = w_ref.shape[1]
    nodes = NODE_DEV
    chunk = 256
    arrived = in_ref[...].reshape(slots, in_ref.shape[2])
    lane_id = iota((8, LANES), 1)
    pick = (lane_id == var_count).astype(F32).astype(BF16)
    node_row = nt_dot(pick, arrived[:, 0:LANES])[0:1, :]
    assign = one_hot(nodes, node_row.astype(jnp.int32) - 1)
    share = 1.0 / jnp.maximum(jnp.sum(assign.astype(F32), axis=1, keepdims=True), 1.0)
    x = arrived[:, m * LANES : m * LANES + var_count]

    def embed(c, e_ref):
        cols = pl.ds(pl.multiple_of(c * chunk, chunk), chunk)
        raw = jnp.dot(x, w_ref[:, cols], preferred_element_type=F32)
        e_ref[...] = (raw + raw * jnp.tanh(raw)).astype(BF16)

    def pool(c, e_ref):
        cols = pl.ds(pl.multiple_of(c * chunk, chunk), chunk)
        pooled_ref[:, cols] = jnp.dot(assign, e_ref[...], preferred_element_type=F32)

    chunks = width // chunk
    embed(0, ea_ref)
    for c in range(chunks):
        here, there = (ea_ref, eb_ref) if c % 2 == 0 else (eb_ref, ea_ref)
        if c + 1 < chunks:
            embed(c + 1, there)
        pool(c, here)
    step = 32
    odd = first_half()[0] == 0
    for r in range(0, HALF_WIN, step):
        lower, upper = slice(r, r + step), slice(HALF_WIN + r, HALF_WIN + r + step)
        halves = []
        for part in (lower, upper):
            summed, part_share = pooled_ref[part, :], share[part]
            centred = summed - jnp.mean(summed, axis=1, keepdims=True)
            variance = jnp.mean(centred * centred, axis=1, keepdims=True) * (part_share * part_share)
            halves.append((centred * (part_share * lax.rsqrt(variance + NORM_EPS))).astype(BF16))
        one_ref[lower, :] = jnp.where(odd, halves[0], halves[1])
        two_ref[lower, :] = jnp.where(odd, halves[1], halves[0])


def qkv_kernel(halves, *refs):
    hidden_refs, (w_ref, qk_ref, vt_ref, rows_ref) = refs[:halves], refs[halves:]
    width = rows_ref.shape[1]
    half = rows_ref.shape[0] // halves
    odd = first_half()[0] == 0
    for i in range(0, halves, 2):
        one, two = hidden_refs[i][...], hidden_refs[i + 1][...]
        rows_ref[i * half : (i + 1) * half, :] = jnp.where(odd, one, two)
        rows_ref[(i + 1) * half : (i + 2) * half, :] = jnp.where(odd, two, one)

    def project(cols):
        return jnp.dot(rows_ref[...], w_ref[:, cols], preferred_element_type=F32).astype(BF16)

    chunk = 512
    for c in range(0, 2 * width, chunk):
        qk_ref[:, c : c + chunk] = project(slice(c, c + chunk))
    for c in range(0, width, chunk):
        vt_ref[c : c + chunk, :] = project(slice(2 * width + c, 2 * width + c + chunk)).T


def attend_kernel(
    var_count, m, left_ref, right_ref, qk_ref, vt_ref, rows_ref, one_ref, two_ref, w_kv_ref, w_out_ref,
    w_dec_ref, *rest,
):
    if m == 0:
        out_ref, kh_ref, vth_ref, att_ref, proc_ref, sa_ref, sb_ref, e_ref, halo_ref = rest
    else:
        dec_ref, in_ref, out_ref, kh_ref, vth_ref, att_ref, proc_ref, sa_ref, sb_ref, e_ref, halo_ref, reply_ref = rest
    half, width = one_ref.shape
    nodes = 2 * half
    head_dim = width // HEADS
    one, two = one_ref[...], two_ref[...]
    odd = first_half()[0] == 0
    halo_ref[0:half, :] = jnp.where(odd, one, two)
    halo_ref[half:, :] = jnp.where(odd, two, one)
    chunk = 256

    def project(c):
        k_src, v_src = slice(width + c, width + c + chunk), slice(2 * width + c, 2 * width + c + chunk)
        kh = jnp.dot(halo_ref[...], w_kv_ref[:, k_src], preferred_element_type=F32)
        kh_ref[:, c : c + chunk] = kh.astype(BF16)
        vh = jnp.dot(halo_ref[...], w_kv_ref[:, v_src], preferred_element_type=F32)
        vth_ref[c : c + chunk, :] = vh.astype(BF16).T

    even = iota((half, LANES), 1) < head_dim
    gain = head_dim ** (-0.5) * 1.4426950408889634
    base = m * nodes

    def scores(p, s_ref):
        cols = slice(p * LANES, (p + 1) * LANES)
        k_cols = slice(width + p * LANES, width + (p + 1) * LANES)
        k_own = qk_ref[base : base + nodes, k_cols]
        for side in range(2):
            row0 = side * half
            q = qk_ref[base + row0 : base + row0 + half, cols]
            none = jnp.zeros_like(q)
            q2 = jnp.concatenate([jnp.where(even, q, none), jnp.where(even, none, q)], axis=0)
            s_all = nt_dot(jnp.concatenate([k_own, kh_ref[row0 : row0 + half, cols]], axis=0), q2)
            s_own, s_halo = s_all[0:nodes], s_all[nodes:]
            if side == 0:
                s_ref[side, 0:half] = s_own[0:half]
                s_ref[side, half:nodes] = s_own[half:] + right_ref[0]
                s_ref[side, nodes:] = s_halo + left_ref[0]
            else:
                s_ref[side, 0:half] = s_own[0:half] + left_ref[1]
                s_ref[side, half:nodes] = s_own[half:]
                s_ref[side, nodes:] = s_halo + right_ref[1]

    def finish(p, s_ref):
        cols = slice(p * LANES, (p + 1) * LANES)
        blocks = (slice(0, half), slice(half, nodes), slice(nodes, nodes + half))
        for side in range(2):
            row0 = side * half
            s0, s1, s2 = (s_ref[side, b] for b in blocks)
            top = jnp.max(jnp.maximum(jnp.maximum(s0, s1), s2), axis=0, keepdims=True)
            total = None
            for b in blocks:
                e = jnp.exp2((s_ref[side, b] - top) * gain)
                e_ref[side, b] = e
                total = e if total is None else total + e
            inv = 1.0 / jnp.sum(total, axis=0, keepdims=True)
            p_own = (e_ref[side, 0:nodes] * inv).astype(BF16)
            p_halo = (e_ref[side, nodes:] * inv).astype(BF16)
            out = jnp.dot(vt_ref[cols, base : base + nodes], p_own, preferred_element_type=F32)
            out += jnp.dot(vth_ref[cols, row0 : row0 + half], p_halo, preferred_element_type=F32)
            pair = jnp.concatenate([out[0:head_dim, 0:half], out[head_dim:, half:]], axis=0)
            att_ref[row0 : row0 + half, cols] = pair.T.astype(BF16)

    if m == 1:
        n_dest = in_ref.shape[0]
        slots = n_dest * CAP
        cube = (n_dest, CAP, LANES)
        asked = in_ref[:, :, LANES:].astype(F32)
        asked = jnp.broadcast_to(asked[:, 0:1, :], cube)
        asked = jnp.where(iota(cube, 2) == iota(cube, 1) + META, asked, 0.0)
        asked = jnp.sum(asked, axis=2, keepdims=True).reshape(slots, 1)
        node_lane = (iota((slots, nodes), 1) + 1).astype(F32)
        reply_ref[...] = (node_lane == asked).astype(F32).astype(BF16)

    pairs = HEADS // 2
    per_chunk = chunk // LANES
    project(0)
    scores(0, sa_ref)
    for p in range(pairs):
        here, there = (sa_ref, sb_ref) if p % 2 == 0 else (sb_ref, sa_ref)
        if p % per_chunk == 0 and p + per_chunk < pairs:
            project((p // per_chunk + 1) * chunk)
        if p + 1 < pairs:
            scores(p + 1, there)
        finish(p, here)

    for c in range(0, width, chunk):
        cols = slice(c, c + chunk)
        mixed = jnp.dot(att_ref[...], w_out_ref[:, cols], preferred_element_type=F32)
        hidden = rows_ref[base : base + nodes, cols].astype(F32)
        proc_ref[:, cols] = (hidden + mixed).astype(BF16)
    decoded = nt_dot(proc_ref[...], w_dec_ref[...]).astype(BF16)
    if m == 0:
        out_ref[...] = jnp.zeros_like(out_ref)
        out_ref[:, 0:var_count] = decoded
    else:
        mine_ref = att_ref.at[:, 0:LANES]
        mine_ref[...] = jnp.zeros_like(mine_ref)
        mine_ref[:, 0:var_count] = decoded
        both = jnp.concatenate([dec_ref[...], mine_ref[...]], axis=1)
        reply = reply_ref[...]
        rows = jnp.dot(reply, both, preferred_element_type=F32).astype(BF16)
        out_ref[...] = rows.reshape(out_ref.shape)


def predict_kernel(var_count, slot_ref, back_ref, x_ref, out_ref):
    n_dest, _, lanes = back_ref.shape
    place = one_hot(n_dest * CAP, slot_ref[...])
    rows = back_ref[...].reshape(n_dest * CAP, lanes)
    got = lax.dot_general(rows, place, TN, preferred_element_type=F32)
    for m in range(x_ref.shape[0]):
        out_ref[m] = (x_ref[m].astype(F32) + got[m * LANES : m * LANES + var_count]).astype(BF16)


def score_kernel(mine_ref, other_ref, target_ref, out_hbm, out_ref, sems):
    refs = [(r, m) for r in (mine_ref, other_ref) for m in range(mine_ref.shape[0])]
    count = len(refs)
    fair_eps = (1.0 - FAIR_ALPHA) / count
    weight = (1.0 - fair_eps) / (2.0 * count * (count - 1)) * 2.0
    edges = [0, 32, 64, out_ref.shape[0]]
    copies = []
    for i, (lo, hi) in enumerate(zip(edges, edges[1:])):
        fields = [r[m, lo:hi].astype(F32) for r, m in refs]
        target = target_ref[lo:hi]
        skill = sum(jnp.abs(f - target) for f in fields) / count
        spread = sum(
            jnp.abs(fields[i] - fields[j]) for i in range(count) for j in range(i + 1, count)
        )
        out_ref[lo:hi] = skill - weight * spread
        rows = pl.ds(lo, hi - lo)
        copies.append(pltpu.make_async_copy(out_ref.at[rows], out_hbm.at[rows], sems.at[i]))
        copies[-1].start()
    for copy in copies:
        copy.wait()


def params(mib=32):
    return pltpu.CompilerParams(vmem_limit_bytes=mib << 20)


def cost(micros):
    return pl.CostEstimate(flops=int(micros * 7e8), bytes_accessed=1 << 20, transcendentals=0)


def on_device(
    initial_states,
    target,
    enc_owner,
    enc_local,
    dec_owner,
    dec_local,
    w_embed,
    w_qkv,
    w_out,
    w_decode,
):
    n_space = lax.axis_size("space")
    members, pts, var_count = initial_states.shape
    width = w_embed.shape[1]
    nodes, half = NODE_DEV, HALF_WIN
    slots = n_space * CAP
    in_hbm = functools.partial(pltpu.with_memory_space_constraint, memory_space=pltpu.HBM)
    rows = [in_hbm(a.reshape(1, pts)) for a in (enc_owner, enc_local, dec_owner, dec_local)]
    wire = jax.ShapeDtypeStruct((n_space, CAP, members * LANES), BF16)

    path = [path_place(b) for b in range(n_space)]
    row_shape = pltpu.VMEM((1, pts), jnp.int32)
    mask = jax.ShapeDtypeStruct((2, half, nodes), F32)
    outgoing, dec_slot, w_enc, states, left, right = pl.pallas_call(
        functools.partial(pack_kernel, var_count),
        in_specs=[HBM_SPEC] * 6,
        out_shape=(
            wire,
            jax.ShapeDtypeStruct((1, pts), jnp.int32),
            jax.ShapeDtypeStruct(w_embed.shape, BF16),
            jax.ShapeDtypeStruct((members, var_count, pts), BF16),
            mask,
            mask,
        ),
        scratch_shapes=[pltpu.VMEM((var_count, members, pts), BF16)]
        + [row_shape] * 4
        + [pltpu.SemaphoreType.DMA((6,))],
        compiler_params=params(),
        cost_estimate=cost(2),
        name="pack",
    )(in_hbm(jnp.transpose(initial_states, (2, 0, 1))), *rows, in_hbm(w_embed))
    arrived = lax.all_to_all(outgoing, "space", 0, 0, tiled=True)

    half_shape = jax.ShapeDtypeStruct((half, width), BF16)
    swaps = [[], []]
    for i, a in enumerate(path):
        b = path[(i + 1) % n_space]
        swaps[i % 2] += [(a, b), (b, a)]
    hidden, halos = [], []
    for m in range(members):
        ends = pl.pallas_call(
            functools.partial(encode_kernel, var_count, m),
            out_shape=(half_shape, half_shape),
            scratch_shapes=[pltpu.VMEM((nodes, width), F32)] + [pltpu.VMEM((slots, 256), BF16)] * 2,
            compiler_params=params(),
            cost_estimate=cost(3),
            name=f"encode{m}",
        )(arrived, w_enc)
        hidden += ends
        halos.append([lax.ppermute(end, "space", swap) for end, swap in zip(ends, swaps)])

    qk, vt, node_rows = pl.pallas_call(
        functools.partial(qkv_kernel, len(hidden)),
        out_shape=(
            jax.ShapeDtypeStruct((members * nodes, 2 * width), BF16),
            jax.ShapeDtypeStruct((width, members * nodes), BF16),
            jax.ShapeDtypeStruct((members * nodes, width), BF16),
        ),
        cost_estimate=cost(5),
        compiler_params=params(),
        name="qkv",
    )(*hidden, w_qkv)

    decoded = None
    for m in range(members):
        extra = () if m == 0 else (decoded, arrived)
        decoded = pl.pallas_call(
            functools.partial(attend_kernel, var_count, m),
            out_shape=jax.ShapeDtypeStruct((nodes, LANES), BF16) if m == 0 else wire,
            scratch_shapes=[
                pltpu.VMEM((nodes, width), BF16),
                pltpu.VMEM((width, nodes), BF16),
                pltpu.VMEM((nodes, width), BF16),
                pltpu.VMEM((nodes, width), BF16),
                pltpu.VMEM((2, nodes + half, nodes), F32),
                pltpu.VMEM((2, nodes + half, nodes), F32),
                pltpu.VMEM((2, nodes + half, nodes), F32),
                pltpu.VMEM((nodes, width), BF16),
            ]
            + [pltpu.VMEM((slots, nodes), BF16)] * m,
            compiler_params=params(),
            cost_estimate=cost(8),
            name=f"attend{m}",
        )(left, right, qk, vt, node_rows, *halos[m], w_qkv, w_out, w_decode.T, *extra)
    replies = decoded

    returned = lax.all_to_all(replies, "space", 0, 0, tiled=True)
    predicted = pl.pallas_call(
        functools.partial(predict_kernel, var_count),
        out_shape=jax.ShapeDtypeStruct((members, var_count, pts), BF16),
        compiler_params=params(),
        name="predict",
    )(dec_slot, returned, states)
    other = lax.ppermute(predicted, "member", [(0, 1), (1, 0)])
    error = pl.pallas_call(
        score_kernel,
        in_specs=[VMEM_SPEC] * 3,
        out_specs=HBM_SPEC,
        out_shape=jax.ShapeDtypeStruct((var_count, pts), F32),
        scratch_shapes=[pltpu.VMEM((var_count, pts), F32), pltpu.SemaphoreType.DMA((3,))],
        compiler_params=params(),
        name="score",
    )(predicted, other, target.T)
    return jnp.transpose(predicted, (0, 2, 1)), error.T


def solution(mesh):
    in_specs = (
        P("member", "space", None),
        P("space", None),
        P("space", None),
        P("space", None),
        P("space", None),
        P("space", None),
        P(),
        P(),
        P(),
        P(),
    )
    out_specs = (P("member", "space", None), P("space", None))
    return jax.shard_map(
        on_device, mesh=mesh, in_specs=in_specs, out_specs=out_specs, check_vma=False
    )
```
